128 devices in a mesh: orb: 8 (over z, core), pair: 16 (over y, x).
Axes of the slice: x: 4, y: 4, z: 4, core: 2. Of those that a mesh axis runs over, the one named last changes fastest.
Arguments:
- blocks: bfloat16 [512, 1024, 320], P(('orb', 'pair')), may hold values from -1.1953125 to 1.1953125
- aux_domain: int32 [512, 1024], replicated, may hold values from 0 to 2047, as said below
- pao_domain: int32 [512, 320], replicated, may hold values from -1 to 639, as said below
- pao_gap: float32 [512, 320], replicated, may hold values from 1 to 4
- amplitudes: bfloat16 [1024, 320, 320], P(('orb', 'pair')), may hold values from -3 to 3
- pair_partner: int32 [1024], replicated, may hold values from 0 to 511, as said below
- coupling_list: int32 [1024, 4], P(('orb', 'pair')), may hold values from 0 to 1023, as said below
- coupling_coef: float32 [1024, 4], P(('orb', 'pair')), may hold values from -0.6 to 0.6
Outputs:
- new_amplitudes: bfloat16 [1024, 320, 320], P(('orb', 'pair'))
- pair_energy: float32 [1024], P(('orb', 'pair'))
- densities: float32 [512, 320, 320], P(('orb', 'pair'))
The draws below stay inside these ranges and needn't reach their ends.
Inputs may be any that keep to these rules, and one draw needn't show every extreme that they name: `aux_domain`: each row holds 1024 distinct auxiliary function ids. `pao_domain`: each row holds distinct PAO ids in its leading slots and -1 in the rest; at least 160 ids a row. With d = p // 8, pair_partner[p] lies in [(d - 1) * 4, (d + 2) * 4). `coupling_list`: row p lists pair ids q with 0 < |q - p| <= 8.
All inputs are finite; a program needn't handle non-finite values.
Results may differ from the reference program's by a relative error of at most 0.003.
Values may be sent and summed in bfloat16 or wider, within the bound.
A program may use at most 128 MiB of HBM per device.

```python
import jax
import jax.numpy as jnp
from jax import lax

NAUX = 1024
NPAO = 320
NAUXG = 2048
NPAOG = 640
OCC_DEV = 4
PAIR_DEV = 8
NCPL = 4
NOCC = 512
NPAIR = 1024


def draw_aux_domain(key, part):
    keys = jax.random.split(key, NOCC)
    rows = jax.vmap(lambda one: jax.random.permutation(one, NAUXG)[:NAUX])(keys)
    return rows.astype(jnp.int32)


def draw_pao_domain(key, part):
    key_perm, key_len = jax.random.split(key)
    keys = jax.random.split(key_perm, NOCC)
    ids = jax.vmap(lambda one: jax.random.permutation(one, NPAOG)[:NPAO])(keys).astype(jnp.int32)
    lens = jax.random.randint(key_len, (NOCC,), NPAO // 2, NPAO + 1)
    lens = lens.at[0].set(NPAO)
    live = jnp.arange(NPAO)[None, :] < lens[:, None]
    return jnp.where(live, ids, -1).astype(jnp.int32)


def draw_pair_partner(key, part):
    pair_ids = jnp.arange(NPAIR)
    lowest = (pair_ids // PAIR_DEV - 1) * OCC_DEV
    offset = jax.random.randint(key, (NPAIR,), 0, 3 * OCC_DEV)
    chosen = lowest + offset
    chosen = jnp.where(chosen < 0, chosen + OCC_DEV, chosen)
    chosen = jnp.where(chosen >= NOCC, chosen - OCC_DEV, chosen)
    return chosen.astype(jnp.int32)


def draw_coupling_list(key, part):
    key_mag, key_sign = jax.random.split(key)
    magnitude = jax.random.randint(key_mag, (NPAIR, NCPL), 1, PAIR_DEV + 1)
    sign = jax.random.randint(key_sign, (NPAIR, NCPL), 0, 2) * 2 - 1
    pair_ids = jnp.arange(NPAIR)[:, None]
    chosen = pair_ids + sign * magnitude
    chosen = jnp.where(chosen < 0, pair_ids + magnitude, chosen)
    chosen = jnp.where(chosen >= NPAIR, pair_ids - magnitude, chosen)
    return chosen.astype(jnp.int32)


def level_of(rng, dims, pieces, least, high):
    def one(dim, parts):
        draws = jax.random.uniform(jax.random.fold_in(jax.random.fold_in(rng, 6), dim), (parts,), jnp.float32, least / len(pieces), high / len(pieces))
        return jnp.repeat(jnp.exp(draws), dims[dim] // parts).reshape((-1,) + (1,) * (len(dims) - dim - 1))

    factor_of = one(*pieces[0])
    for cut in pieces[1:]:
        factor_of = factor_of * one(*cut)
    return factor_of


def centred(key, extent, deviation, bound, pieces=(), held_as=jnp.bfloat16):
    array = jax.random.normal(key, extent, jnp.float32) * deviation
    if len(pieces) > 0:
        array = level_of(key, extent, pieces, -0.22, 0.18) * array
    return jnp.clip(array, min=-bound, max=bound).astype(held_as)


def setup_inputs(seed: int = 0) -> dict:
    seeds = jax.random.split(jax.random.key(seed), 9)
    blocks = centred(seeds[0], (NOCC, NAUX, NPAO), 0.2, 1.1953125, ((0, 128),))
    aux_domain = draw_aux_domain(jax.random.fold_in(seeds[8], 71), 0)
    pao_domain = draw_pao_domain(jax.random.fold_in(seeds[8], 71), 0)
    pao_gap = jnp.clip(jax.random.uniform(seeds[3], (NOCC, NPAO), jnp.float32, 1.0, 4.0), 1.0, 4.0)
    amplitudes = centred(seeds[4], (NPAIR, NPAO, NPAO), 0.5, 3.0, ((0, 128),))
    pair_partner = draw_pair_partner(jax.random.fold_in(seeds[8], 71), 0)
    coupling_list = draw_coupling_list(jax.random.fold_in(seeds[8], 71), 0)
    coupling_coef = jnp.clip(jax.random.uniform(seeds[7], (NPAIR, NCPL), jnp.float32, -0.6, 0.6) * level_of(seeds[7], (NPAIR, NCPL), ((0, 128),), -0.4, 0.0), -0.6, 0.6)
    return {"blocks": blocks, "aux_domain": aux_domain, "pao_domain": pao_domain, "pao_gap": pao_gap, "amplitudes": amplitudes, "pair_partner": pair_partner, "coupling_list": coupling_list, "coupling_coef": coupling_coef}


def first_orbital(pair_id):
    return ((pair_id // PAIR_DEV) * OCC_DEV + pair_id % OCC_DEV).astype(jnp.int32)


def inverse_map(domain, width):
    places = jnp.where(domain >= 0, domain, width)
    return jnp.full((width,), -1, jnp.int32).at[places].set(jnp.arange(domain.shape[0], dtype=jnp.int32), mode="drop")


def lookup(table, ids):
    found = table[jnp.clip(ids, 0, table.shape[0] - 1)]
    return jnp.where(ids >= 0, found, -1).astype(jnp.int32)


def take_rows(block, index):
    rows = jnp.take(block, jnp.clip(index, 0, block.shape[0] - 1), axis=0)
    keep = (index >= 0).reshape((-1,) + (1,) * (block.ndim - 1))
    return jnp.where(keep, rows, jnp.zeros_like(rows))


def pair_terms(left_block, right_block, aux_left, aux_right, pao_left, pao_right, gap_left, gap_right, amp, near_amps, near_left, near_right, coefs):
    index = lookup(inverse_map(aux_right, NAUXG), aux_left)
    aligned = take_rows(right_block, index)
    mask_left = (pao_left >= 0).astype(jnp.float32)
    mask_right = (pao_right >= 0).astype(jnp.float32)
    both = mask_left[:, None] * mask_right[None, :]
    exchange = lax.dot_general(left_block, aligned, (((0,), (0,)), ((), ())), preferred_element_type=jnp.float32) * both
    masked = (amp.astype(jnp.float32) * both).astype(jnp.bfloat16)

    def project(near_amp, pao_near_left, pao_near_right, coef):
        rows = lookup(inverse_map(pao_near_left, NPAOG), pao_left)
        cols = lookup(inverse_map(pao_near_right, NPAOG), pao_right)
        picked = take_rows(near_amp, rows)
        picked = take_rows(picked.T, cols).T
        return coef * picked.astype(jnp.float32)

    coupling = jnp.sum(jax.vmap(project)(near_amps, near_left, near_right, coefs), axis=0)
    denom = gap_left[:, None] + gap_right[None, :]
    masked_f = masked.astype(jnp.float32)
    residual = exchange + denom * masked_f - coupling
    new_amp = (masked_f - 0.5 * residual / denom).astype(jnp.bfloat16)
    energy = jnp.sum(exchange * masked_f) / masked.shape[0]
    return new_amp, energy, masked


def left_density(masked):
    return jnp.dot(masked, masked.T, preferred_element_type=jnp.float32) / masked.shape[0]


def right_density(masked):
    return lax.dot_general(masked, masked, (((0,), (0,)), ((), ())), preferred_element_type=jnp.float32) / masked.shape[0]


def reference(blocks, aux_domain, pao_domain, pao_gap, amplitudes, pair_partner, coupling_list, coupling_coef):
    pair_ids = jnp.arange(NPAIR, dtype=jnp.int32)

    def step(dens, items):
        pair_id, amp, neighbours, coefs = items
        left = first_orbital(pair_id)
        right = pair_partner[pair_id]
        new_amp, energy, masked = pair_terms(blocks[left], blocks[right], aux_domain[left], aux_domain[right], pao_domain[left], pao_domain[right], pao_gap[left], pao_gap[right], amp, amplitudes[neighbours], pao_domain[first_orbital(neighbours)], pao_domain[pair_partner[neighbours]], coefs)
        dens = dens.at[left].add(left_density(masked))
        dens = dens.at[right].add(right_density(masked))
        return dens, (new_amp, energy)

    start = jnp.zeros((NOCC, NPAO, NPAO), jnp.float32)
    dens, (new_amps, energies) = lax.scan(step, start, (pair_ids, amplitudes, coupling_list, coupling_coef))
    return new_amps, energies, dens
```

```python
import functools

import jax
import jax.numpy as jnp
from jax import lax
from jax.experimental import pallas as pl
from jax.experimental.pallas import tpu as pltpu
from jax.sharding import PartitionSpec as P


OCC_DEV = 4
PAIR_DEV = 8
NCPL = 4
AXES = ("orb", "pair")
F32 = jnp.float32
BF16 = jnp.bfloat16
MAIN = 256
CUTS = (0, 1, 3, 4)
ORDER_START, ORDER_COUNT, ORDER_SIZE = 16, 24, 32
CONTRACT_LAST = (((1,), (1,)), ((), ()))


def column(row, rows):
    wide = jnp.broadcast_to(row, (128, row.shape[1]))
    return wide.T[:rows]


def wanted(row):
    return jnp.where(row < 0, -2, row)


def lanes(col, row):
    pieces = [
        jnp.where(col == row[:, at : at + 128], F32(1), F32(0)).astype(BF16)
        for at in range(0, row.shape[1], 128)
    ]
    return pieces[0] if len(pieces) == 1 else jnp.concatenate(pieces, axis=1)


def mask_kernel(here, partner, tab_ref, low_ref, high_ref, out_ref, *, base_of):
    k = pl.program_id(0)
    rows = low_ref.shape[1]
    first = here[0] * OCC_DEV + k - base_of(here[0])
    left = column(tab_ref[pl.ds(first, 1), :], rows) >= 0

    def masked(amp, p, start, size):
        at = partner[here[0] * PAIR_DEV + p] - base_of(here[0])
        right = tab_ref[pl.ds(at, 1), :][:, start : start + size] >= 0
        keep = left[:, :1] & right
        return jnp.where(keep, amp[0, :, start : start + size].astype(F32), F32(0))

    rests = []
    for n, ref in enumerate((low_ref, high_ref)):
        p = k + n * OCC_DEV
        out_ref[0, :, n * MAIN : (n + 1) * MAIN] = masked(ref, p, 0, MAIN).astype(BF16)
        rests.append(masked(ref, p, MAIN, rows - MAIN))
    out_ref[0, :, 2 * MAIN :] = jnp.concatenate(rests, axis=1).astype(BF16)


def stage_of(spot):
    slot = lax.rem(spot, OCC_DEV)
    away = (spot // OCC_DEV) != 1
    return jnp.where(away & (slot >= CUTS[1]), jnp.where(slot >= CUTS[2], 2, 1), 0)


def align_kernel(here, partner, aux_ref, left_ref, out_ref, order_ref, col_ref, *, base_of):
    p = pl.program_id(0)

    @pl.when(p == 0)
    def _():
        total = jnp.int32(0)
        for stage in range(len(CUTS) - 1):
            start = total
            for q in range(PAIR_DEV):
                spot = partner[here[0] * PAIR_DEV + q] - (here[0] - 1) * OCC_DEV
                hit = stage_of(spot) == stage
                order_ref[jnp.where(hit, total, PAIR_DEV)] = q
                total = total + hit.astype(jnp.int32)
            order_ref[ORDER_COUNT + stage] = jnp.maximum(total - start, 1)
            order_ref[ORDER_START + stage] = start

    k = lax.rem(p, OCC_DEV)
    naux = left_ref.shape[2]
    base = base_of(here[0])
    first = here[0] * OCC_DEV + k - base
    col_ref[...] = column(aux_ref[pl.ds(first, 1), :], naux)
    second = partner[here[0] * PAIR_DEV + p] - base
    left = left_ref[0]
    present = aux_ref[pl.ds(second, 1), :]
    for at in range(0, naux, MAIN):
        pick = lanes(col_ref[...], present[:, at : at + MAIN])
        out_ref[0, :, at : at + MAIN] = jnp.dot(left, pick, preferred_element_type=F32).astype(BF16)


def coupling_kernel(
    here,
    partner,
    near,
    coef,
    tab_ref,
    prev_hbm,
    own_hbm,
    next_hbm,
    out_ref,
    dens_ref,
    amps,
    rows_ref,
    cols_ref,
    acc,
    sems,
    *,
    base_of,
):
    p = pl.program_id(0)
    me = here[0]
    base = base_of(me)
    rows = acc.shape[1]
    rest = rows - MAIN

    @pl.when(p == 0)
    def _():
        copies = [
            pltpu.make_async_copy(ref, amps.at[s], sems.at[s])
            for s, ref in enumerate((prev_hbm, own_hbm, next_hbm))
        ]
        for c in copies:
            c.start()
        for c in copies:
            c.wait()
        for o in range(OCC_DEV):
            packed = amps[1, o]
            acc[o] = lax.dot_general(packed, packed, CONTRACT_LAST, preferred_element_type=F32)

    low = lax.broadcasted_iota(jnp.int32, (1, 2 * rest), 1) < rest
    k = lax.rem(p, OCC_DEV)
    left = column(wanted(tab_ref[pl.ds(me * OCC_DEV + k - base, 1), :]), rows)
    right = column(
        wanted(tab_ref[pl.ds(partner[me * PAIR_DEV + p] - base, 1), :]), rows
    )
    held_rest, held_row = None, None
    for c in range(NCPL):
        m = near[p * NCPL + c]
        spot = m - (me - 1) * PAIR_DEV
        side, inner = spot // PAIR_DEV, lax.rem(spot, PAIR_DEV)
        slot, half = lax.rem(inner, OCC_DEV), inner // OCC_DEV
        i_m = (m // PAIR_DEV) * OCC_DEV + lax.rem(m, OCC_DEV) - base
        j_m = partner[m] - base
        scale = coef[p * NCPL + c]
        pick = lanes(left, tab_ref[pl.ds(i_m, 1), :])[:, :rows]
        main = amps[side, slot, :, pl.ds(pl.multiple_of(half * MAIN, MAIN), MAIN)]
        tail = amps[side, slot, :, 2 * MAIN :]
        got = jnp.dot(pick, main, preferred_element_type=F32) * scale
        rows_ref[:, c * MAIN : (c + 1) * MAIN] = got.astype(BF16)
        got = jnp.dot(pick, tail, preferred_element_type=F32) * scale
        got = jnp.where(half == c % 2, got, pltpu.roll(got, rest, 1))
        row = tab_ref[pl.ds(j_m, 1), :]
        cols_ref[:, c * MAIN : (c + 1) * MAIN] = lanes(right, row[:, :MAIN])
        row = row[:, MAIN:]
        if c % 2 == 0:
            held_rest, held_row = got, row
        else:
            at = NCPL * MAIN + (c // 2) * 2 * rest
            rows_ref[:, at : at + 2 * rest] = jnp.where(low, held_rest, got).astype(BF16)
            cols_ref[:, at : at + 2 * rest] = lanes(right, jnp.where(low, held_row, row))
    out_ref[0] = lax.dot_general(
        rows_ref[...], cols_ref[...], CONTRACT_LAST, preferred_element_type=F32
    )

    half = p // OCC_DEV
    for side in range(3):
        q = (me - 1 + side) * PAIR_DEV + p
        inside = (q >= 0) & (q < partner.shape[0])
        o = partner[jnp.clip(q, 0, partner.shape[0] - 1)] - me * OCC_DEV

        @pl.when(inside & (o >= 0) & (o < OCC_DEV))
        def _(side=side, o=o):
            main = amps[side, k, :, pl.ds(pl.multiple_of(half * MAIN, MAIN), MAIN)]
            tail = amps[side, k, :, 2 * MAIN :].astype(F32)
            tail = jnp.where(half == 0, tail, pltpu.roll(tail, rest, 1))
            whole = jnp.concatenate([main, tail[:, :rest].astype(BF16)], axis=1)
            acc[o] += lax.dot_general(
                whole, whole, (((0,), (0,)), ((), ())), preferred_element_type=F32
            )

    @pl.when(p == PAIR_DEV - 1)
    def _():
        dens_ref[...] = acc[...] / rows


def turn(order, stage, s):
    at = order[ORDER_START + stage] + s
    return order[jnp.minimum(at, PAIR_DEV - 1)]


def final_kernel(here, partner, order, *refs, base_of, stage):
    sources = len(CUTS[: stage + 2]) - 1
    tab_ref, gap_ref, picked_hbm, own_hbm = refs[:4]
    halos = refs[4 : 4 + 2 * sources]
    coupling_hbm, amp_hbm = refs[4 + 2 * sources : 6 + 2 * sources]
    rest_refs = refs[6 + 2 * sources :]
    if stage:
        before_ref, rest_refs = rest_refs[1], rest_refs[2:]
    new_hbm, energy_ref, block, picked, coupling, amps, new, sems, out_sems = rest_refs
    me = here[0]
    base = base_of(me)
    rows = new.shape[1]
    rest = rows - MAIN
    count = order[ORDER_COUNT + stage]

    def fetch(step, act):
        q = turn(order, stage, step)
        at = lax.rem(step, 2)
        spot = partner[me * PAIR_DEV + q] - (me - 1) * OCC_DEV
        slot, side = lax.rem(spot, OCC_DEV), spot // OCC_DEV
        act(pltpu.make_async_copy(picked_hbm.at[q], picked.at[at], sems.at[at, 1]))
        act(pltpu.make_async_copy(coupling_hbm.at[q], coupling.at[at], sems.at[at, 2]))
        act(pltpu.make_async_copy(amp_hbm.at[lax.rem(q, OCC_DEV)], amps.at[at], sems.at[at, 3]))

        def copy(ref, index):
            return pltpu.make_async_copy(ref.at[index], block.at[at], sems.at[at, 0])

        here_now = (side == 1) | (slot >= CUTS[sources])

        @pl.when(here_now)
        def _():
            act(copy(own_hbm, slot))

        for n in range(sources):
            for w, far in enumerate((0, 2)):

                @pl.when((side == far) & (slot >= CUTS[n]) & (slot < CUTS[n + 1]))
                def _(n=n, w=w):
                    act(copy(halos[2 * n + w], slot - CUTS[n]))

    def store(step):
        at = lax.rem(step, 2)
        return pltpu.make_async_copy(
            new.at[at], new_hbm.at[turn(order, stage, step)], out_sems.at[at]
        )

    fetch(0, lambda c: c.start())
    for q in range(PAIR_DEV):
        energy_ref[q] = before_ref[q] if stage else F32(0)

    @pl.loop(0, count)
    def _(s):
        @pl.when(s + 1 < count)
        def _():
            fetch(s + 1, lambda c: c.start())

        fetch(s, lambda c: c.wait())
        at = lax.rem(s, 2)

        @pl.when(s >= 2)
        def _():
            store(s - 2).wait()

        p = turn(order, stage, s)
        k, half = lax.rem(p, OCC_DEV), p // OCC_DEV
        first = me * OCC_DEV + k - base
        second = partner[me * PAIR_DEV + p] - base
        keep_left = column(tab_ref[pl.ds(first, 1), :], rows)[:, :1] >= 0
        gap_left = column(gap_ref[pl.ds(first, 1), :], rows)[:, :1]
        whole = lax.dot_general(picked[at], block[at], CONTRACT_LAST, preferred_element_type=F32)
        tail = amps[at, :, 2 * MAIN :].astype(F32)
        tail = jnp.where(half == 0, tail, pltpu.roll(tail, rest, 1))
        main = amps[at, :, pl.ds(pl.multiple_of(half * MAIN, MAIN), MAIN)].astype(F32)
        energy = F32(0)
        for start, size, amp in ((0, MAIN, main), (MAIN, rest, tail[:, :rest])):
            part = slice(start, start + size)
            keep = keep_left & (tab_ref[pl.ds(second, 1), :][:, part] >= 0)
            exchange = jnp.where(keep, whole[:, part], F32(0))
            denom = gap_left + gap_ref[pl.ds(second, 1), :][:, part]
            residual = exchange + denom * amp - coupling[at, :, part]
            new[at, :, part] = (amp - 0.5 * residual / denom).astype(BF16)
            energy += jnp.sum(exchange * amp)
        energy_ref[p] = energy / rows
        store(s).start()

    @pl.when(count >= 2)
    def _():
        store(count - 2).wait()

    store(count - 1).wait()


def whole_spec(shape):
    return pl.BlockSpec(shape, lambda *_: (0,) * len(shape))


def any_spec():
    return pl.BlockSpec(memory_space=pltpu.MemorySpace.HBM)


def call(kernel, prefetch, grid, ins, outs, scratch, args, flops, nbytes, aliases=None):
    return pl.pallas_call(
        kernel,
        out_shape=[s for s, _ in outs],
        grid_spec=pltpu.PrefetchScalarGridSpec(
            num_scalar_prefetch=len(prefetch),
            grid=grid,
            in_specs=ins,
            out_specs=[s for _, s in outs],
            scratch_shapes=scratch,
        ),
        cost_estimate=pl.CostEstimate(flops=flops, bytes_accessed=nbytes, transcendentals=0),
        compiler_params=pltpu.CompilerParams(vmem_limit_bytes=56 * 1024 * 1024),
        input_output_aliases=aliases or {},
    )(*prefetch, *args)


def neighbours(x):
    devices = lax.axis_size(AXES)
    up = [(i, i + 1) for i in range(devices - 1)]
    down = [(i + 1, i) for i in range(devices - 1)]
    before = lax.ppermute(x, AXES, up)
    after = lax.ppermute(x, AXES, down)
    return before, after


def local(
    blocks, aux_domain, pao_domain, pao_gap, amplitudes, pair_partner, coupling_list, coupling_coef
):
    here = lax.axis_index(AXES).astype(jnp.int32)
    norb, naux = aux_domain.shape
    npao = pao_domain.shape[1]
    span_aux, span_pao = 3 * OCC_DEV, 5 * OCC_DEV

    def base_aux(h):
        return jnp.clip((h - 1) * OCC_DEV, 0, norb - span_aux)

    def base_pao(h):
        return jnp.clip((h - 2) * OCC_DEV, 0, norb - span_pao)

    tab = lax.dynamic_slice(pao_domain, (base_pao(here), 0), (span_pao, npao))
    tab = jnp.concatenate([tab, tab[:, MAIN:]], axis=1)
    gap = lax.dynamic_slice(pao_gap, (base_pao(here), 0), (span_pao, npao))
    gap = jnp.concatenate([gap, gap[:, MAIN:]], axis=1)
    aux = lax.dynamic_slice(aux_domain, (base_aux(here), 0), (span_aux, naux))
    me = here[None]
    flat_near = coupling_list.reshape(-1)
    flat_coef = coupling_coef.reshape(-1)
    turned = jnp.swapaxes(blocks, 1, 2)
    packed_shape = (OCC_DEV, npao, 2 * npao)
    hbm = any_spec()
    sds = jax.ShapeDtypeStruct
    wide = tab.shape[1]

    halos = [neighbours(turned[CUTS[0] : CUTS[1]])]
    (packed,) = call(
        functools.partial(mask_kernel, base_of=base_pao),
        (me, pair_partner),
        (OCC_DEV,),
        [
            whole_spec((span_pao, wide)),
            pl.BlockSpec((1, npao, npao), lambda k, *_: (k, 0, 0)),
            pl.BlockSpec((1, npao, npao), lambda k, *_: (k + OCC_DEV, 0, 0)),
        ],
        [
            (
                sds(packed_shape, BF16),
                pl.BlockSpec((1, npao, 2 * npao), lambda k, *_: (k, 0, 0)),
            )
        ],
        [],
        (tab, amplitudes, amplitudes),
        1000,
        4_000_000,
    )
    amp_prev, amp_next = neighbours(packed)
    picked, order = call(
        functools.partial(align_kernel, base_of=base_aux),
        (me, pair_partner),
        (PAIR_DEV,),
        [
            whole_spec((span_aux, naux)),
            pl.BlockSpec((1, npao, naux), lambda p, *_: (lax.rem(p, OCC_DEV), 0, 0)),
        ],
        [
            (
                sds((PAIR_DEV, npao, naux), BF16),
                pl.BlockSpec((1, npao, naux), lambda p, *_: (p, 0, 0)),
            ),
            (
                sds((ORDER_SIZE,), jnp.int32),
                pl.BlockSpec(memory_space=pltpu.MemorySpace.SMEM),
            ),
        ],
        [pltpu.VMEM((naux, 128), jnp.int32)],
        (aux, turned),
        2 * PAIR_DEV * npao * naux * naux,
        8_000_000,
    )
    later, order = lax.optimization_barrier((turned[CUTS[1] : CUTS[2]], order))
    halos.append(neighbours(later))
    amp_prev, amp_next, later = lax.optimization_barrier((amp_prev, amp_next, turned[CUTS[2] :]))
    halos.append(neighbours(later))
    coupling, densities = call(
        functools.partial(coupling_kernel, base_of=base_pao),
        (me, pair_partner, flat_near, flat_coef),
        (PAIR_DEV,),
        [whole_spec((span_pao, wide)), hbm, hbm, hbm],
        [
            (
                sds((PAIR_DEV, npao, npao), F32),
                pl.BlockSpec((1, npao, npao), lambda p, *_: (p, 0, 0)),
            ),
            (sds((OCC_DEV, npao, npao), F32), whole_spec((OCC_DEV, npao, npao))),
        ],
        [
            pltpu.VMEM((3,) + packed_shape, BF16),
            pltpu.VMEM((npao, NCPL * npao), BF16),
            pltpu.VMEM((npao, NCPL * npao), BF16),
            pltpu.VMEM((OCC_DEV, npao, npao), F32),
            pltpu.SemaphoreType.DMA((3,)),
        ],
        (tab, amp_prev, packed, amp_next),
        2 * PAIR_DEV * (2 * NCPL + 2) * npao**3,
        12_000_000,
    )
    done = ()
    for stage in range(len(halos)):
        arrived = [x for pair in halos[: stage + 1] for x in pair]
        smem = pl.BlockSpec(memory_space=pltpu.MemorySpace.SMEM)
        vmem = pl.BlockSpec(memory_space=pltpu.MemorySpace.VMEM)
        inputs = (tab, gap, picked, turned, *arrived, coupling, packed)
        done = call(
            functools.partial(final_kernel, base_of=base_pao, stage=stage),
            (me, pair_partner, order),
            (),
            [vmem, vmem] + [hbm] * (len(inputs) - 2) + ([hbm, smem] if stage else []),
            [(sds((PAIR_DEV, npao, npao), BF16), hbm), (sds((PAIR_DEV,), F32), smem)],
            [
                pltpu.VMEM((2, npao, naux), BF16),
                pltpu.VMEM((2, npao, naux), BF16),
                pltpu.VMEM((2, npao, npao), F32),
                pltpu.VMEM((2, npao, 2 * npao), BF16),
                pltpu.VMEM((2, npao, npao), BF16),
                pltpu.SemaphoreType.DMA((2, 4)),
                pltpu.SemaphoreType.DMA((2,)),
            ],
            inputs + tuple(done),
            PAIR_DEV * npao * npao * naux,
            8_000_000,
            {3 + len(inputs): 0} if stage else None,
        )
    new_amps, energies = done
    return (new_amps, energies, densities)


def solution(mesh):
    return jax.shard_map(
        local,
        mesh=mesh,
        in_specs=(
            P(("orb", "pair"), None, None),
            P(),
            P(),
            P(),
            P(("orb", "pair"), None, None),
            P(),
            P(("orb", "pair"), None),
            P(("orb", "pair"), None),
        ),
        out_specs=(
            P(("orb", "pair"), None, None),
            P(("orb", "pair")),
            P(("orb", "pair"), None, None),
        ),
        check_vma=False,
    )
```

```python
import functools

import jax
import jax.numpy as jnp
from jax import lax
from jax.experimental import pallas as pl
from jax.experimental.pallas import tpu as pltpu
from jax.sharding import PartitionSpec as P

OCC_DEV = 4
PAIR_DEV = 8
NCPL = 4
F32 = jnp.float32
BF16 = jnp.bfloat16
MAIN = 256
LANE = 128
MESH = pl.DeviceIdType.MESH
CONTRACT_LAST = (((1,), (1,)), ((), ()))
CONTRACT_FIRST = (((0,), (0,)), ((), ()))
CUTS = ((0, 256), (256, 768), (768, 1024))


def column(row, rows):
    wide = jnp.broadcast_to(row, (LANE, row.shape[1]))
    return wide.T[:rows]


def wanted(row):
    return jnp.where(row < 0, -2, row)


def lanes(col, row):
    pieces = [
        jnp.where(col == row[:, at : at + LANE], F32(1), F32(0)).astype(BF16)
        for at in range(0, row.shape[1], LANE)
    ]
    return pieces[0] if len(pieces) == 1 else jnp.concatenate(pieces, axis=1)


def wrapped(index, length):
    return lax.rem(lax.rem(index, length) + length, length)


def dot(a, b, dims=(((1,), (0,)), ((), ()))):
    return lax.dot_general(a, b, dims, preferred_element_type=F32)


def kernel(
    devices,
    partner,
    near,
    coef,
    blocks_hbm,
    aux_hbm,
    pao_hbm,
    gap_hbm,
    amps_hbm,
    new_hbm,
    energy_ref,
    dens_hbm,
    own,
    aux,
    pao_window,
    gap_window,
    raw,
    tab,
    gap,
    amps,
    picked,
    part0,
    part1,
    part2,
    exch,
    scale_ref,
    base_ref,
    rows_ref,
    cols_ref,
    acc,
    new,
    local_sems,
    send_sems,
    recv_sems,
    out_sems,
):
    pairs_axis = lax.axis_size("pair")
    me = lax.axis_index("orb") * pairs_axis + lax.axis_index("pair")
    npao, naux = own.shape[1:]
    norb = aux_hbm.shape[0]
    rest = npao - MAIN
    parts = (part0, part1, part2)
    has = (me > 0, me < devices - 1)
    peers = tuple(
        (lax.div(at, pairs_axis), lax.rem(at, pairs_axis))
        for at in (lax.rem(me + devices - 1, devices), lax.rem(me + 1, devices))
    )

    groups = norb // 8
    group = me // 2
    aux_start = (group - 1) * 8
    loads = [
        pltpu.make_async_copy(src, dst, local_sems.at[n])
        for n, (src, dst) in enumerate(
            (
                (pao_hbm, pao_window),
                (amps_hbm, raw),
                (blocks_hbm, own),
                (gap_hbm, gap_window),
                (blocks_hbm.at[:, :, CUTS[0][0] : CUTS[0][1]], part0.at[1]),
                (blocks_hbm.at[:, :, CUTS[1][0] : CUTS[1][1]], part1.at[1]),
                (blocks_hbm.at[:, :, CUTS[2][0] : CUTS[2][1]], part2.at[1]),
                *[
                    (
                        aux_hbm.at[pl.ds(lax.rem(group + groups - 1 + g, groups) * 8, 8)],
                        aux.at[8 * g : 8 * g + 8],
                    )
                    for g in range(3)
                ],
            )
        )
    ]
    for copy in loads:
        copy.start()

    barrier = pltpu.get_barrier_semaphore()
    for side in range(2):

        @pl.when(has[side])
        def _(side=side):
            pl.semaphore_signal(barrier, inc=1, device_id=peers[side], device_id_type=MESH)

    inner = jnp.logical_and(*has)

    @pl.when(inner)
    def _():
        pl.semaphore_wait(barrier, 2)

    @pl.when(jnp.logical_not(inner))
    def _():
        pl.semaphore_wait(barrier, 1)

    def remote(n, side):
        if n < len(CUTS):
            src = blocks_hbm.at[:, :, CUTS[n][0] : CUTS[n][1]]
            dst = parts[n].at[2 - 2 * side]
        else:
            src, dst = amps.at[1], amps.at[2 - 2 * side]
        return pltpu.make_async_remote_copy(
            src_ref=src,
            dst_ref=dst,
            send_sem=send_sems.at[n, side],
            recv_sem=recv_sems.at[n, side],
            device_id=peers[side],
            device_id_type=MESH,
        )

    def start(n):
        for side in range(2):

            @pl.when(has[side])
            def _(side=side):
                remote(n, side).start()

    def sent(n):
        for side in range(2):

            @pl.when(has[side])
            def _(side=side):
                remote(n, side).wait_send()

    def arrived(n):
        for side in range(2):

            @pl.when(has[1 - side])
            def _(side=side):
                remote(n, side).wait_recv()

    start(0)

    def rows_of(window):
        x = window[...]
        return jnp.concatenate([x, x[MAIN:]], axis=0).T

    loads[0].wait()
    tab[...] = rows_of(pao_window)
    loads[1].wait()
    first = me * OCC_DEV

    @pl.loop(0, OCC_DEV)
    def _(k):
        left = column(tab[pl.ds(first + k, 1), :], npao)[:, :1] >= 0
        tails = []
        for n in range(2):
            p = k + n * OCC_DEV
            at = partner[me * PAIR_DEV + p]
            keep = left & (tab[pl.ds(at, 1), :] >= 0)[:, :npao]
            amp = jnp.where(keep, raw[p].astype(F32), F32(0))
            amps[1, k, :, n * MAIN : (n + 1) * MAIN] = amp[:, :MAIN].astype(BF16)
            tails.append(amp[:, MAIN:])
        amps[1, k, :, 2 * MAIN :] = jnp.concatenate(tails, axis=1).astype(BF16)

    loads[3].wait()
    gap[...] = rows_of(gap_window)
    for side in range(2):

        @pl.when(jnp.logical_not(has[side]))
        def _(side=side):
            amps[2 * side] = jnp.zeros_like(amps[2 * side])

    loads[2].wait()
    for g in range(3):
        loads[7 + g].wait()

    def align(p):
        k = lax.rem(p, OCC_DEV)
        col = column(aux[pl.ds(me * OCC_DEV + k - aux_start, 1), :], naux)
        second = wrapped(partner[me * PAIR_DEV + p] - aux_start, aux.shape[0])
        present = aux[pl.ds(second, 1), :]
        for at in range(0, naux, MAIN):
            pick = lanes(col, present[:, at : at + MAIN])
            picked[p, :, at : at + MAIN] = dot(own[k], pick).astype(BF16)

    pl.loop(0, 1)(align)
    start(3)
    pl.loop(1, PAIR_DEV)(align)

    def amp_of(side, p):
        k, half = lax.rem(p, OCC_DEV), lax.div(p, OCC_DEV)
        main = amps[side, k, :, pl.ds(pl.multiple_of(half * MAIN, MAIN), MAIN)]
        tail = amps[side, k, :, 2 * MAIN :].astype(F32)
        tail = jnp.where(half == 0, tail, pltpu.roll(tail, rest, 1))
        return main, tail[:, :rest]

    def right_terms(side):
        @pl.loop(0, PAIR_DEV)
        def _(p):
            q = lax.rem((me + devices - 1 + side) * PAIR_DEV + p, devices * PAIR_DEV)
            target = partner[q] - me * OCC_DEV
            main, tail = amp_of(side, p)
            whole = jnp.concatenate([main, tail.astype(BF16)], axis=1)
            term = dot(whole, whole, CONTRACT_FIRST)
            for o in range(OCC_DEV):
                acc[o] += jnp.where(target == o, F32(1), F32(0)) * term

    for o in range(OCC_DEV):
        packed = amps[1, o]
        acc[o] = dot(packed, packed, CONTRACT_LAST)
    right_terms(1)

    def block_of(part, p):
        spot = wrapped(partner[me * PAIR_DEV + p] - (me - 1) * OCC_DEV, 3 * OCC_DEV)
        return part[lax.div(spot, OCC_DEV), lax.rem(spot, OCC_DEV)]

    def exchange_term(n, p):
        lo, hi = CUTS[n]
        return dot(picked[p, :, lo:hi], block_of(parts[n], p), CONTRACT_LAST)

    loads[4].wait()
    arrived(0)

    @pl.loop(0, PAIR_DEV)
    def _(p):
        exch[p] = exchange_term(0, p)

    sent(3)
    start(1)
    arrived(3)
    low = lax.broadcasted_iota(jnp.int32, (1, 2 * rest), 1) < rest

    @pl.loop(0, PAIR_DEV)
    def _(p):
        i_row = me * OCC_DEV + lax.rem(p, OCC_DEV)
        j_row = partner[me * PAIR_DEV + p]
        left = column(wanted(tab[pl.ds(i_row, 1), :]), npao)
        right = column(wanted(tab[pl.ds(j_row, 1), :]), npao)
        held_rest, held_row = None, None
        for c in range(NCPL):
            m = near[c, p]
            spot = wrapped(m - (me - 1) * PAIR_DEV, 3 * PAIR_DEV)
            side, inner = lax.div(spot, PAIR_DEV), lax.rem(spot, PAIR_DEV)
            slot, half = lax.rem(inner, OCC_DEV), lax.div(inner, OCC_DEV)
            i_m = lax.div(m, PAIR_DEV) * OCC_DEV + slot
            j_m = partner[m]
            scale = coef[c, p]
            pick = lanes(left, tab[pl.ds(i_m, 1), :])[:, :npao]
            both = amps[side, slot]
            main = jnp.where(half == 0, both[:, :MAIN], both[:, MAIN : 2 * MAIN])
            tail = both[:, 2 * MAIN :]
            rows_ref[:, c * MAIN : (c + 1) * MAIN] = (dot(pick, main) * scale).astype(BF16)
            got = dot(pick, tail) * scale
            got = jnp.where(half == c % 2, got, pltpu.roll(got, rest, 1))
            row = tab[pl.ds(j_m, 1), :]
            cols_ref[:, c * MAIN : (c + 1) * MAIN] = lanes(right, row[:, :MAIN])
            row = row[:, MAIN:]
            if c % 2 == 0:
                held_rest, held_row = got, row
            else:
                at = NCPL * MAIN + (c // 2) * 2 * rest
                rows_ref[:, at : at + 2 * rest] = jnp.where(low, held_rest, got).astype(BF16)
                cols_ref[:, at : at + 2 * rest] = lanes(right, jnp.where(low, held_row, row))
        coupling = dot(rows_ref[...], cols_ref[...], CONTRACT_LAST)
        gap_left = column(gap[pl.ds(i_row, 1), :], npao)[:, :1]
        gap_right = gap[pl.ds(j_row, 1), :]
        keep_right = tab[pl.ds(j_row, 1), :] >= 0
        main, tail = amp_of(1, p)
        for lo, hi, amp in ((0, MAIN, main.astype(F32)), (MAIN, npao, tail)):
            keep = (left[:, :1] >= 0) & keep_right[:, lo:hi]
            denom = gap_left + gap_right[:, lo:hi]
            half_inverse = 0.5 / denom
            scale_ref[p, :, lo:hi] = jnp.where(keep, half_inverse, F32(0))
            base_ref[p, :, lo:hi] = amp - (denom * amp - coupling[:, lo:hi]) * half_inverse

    start(2)
    right_terms(0)
    right_terms(2)
    acc[...] = acc[...] / npao
    dens_out = pltpu.make_async_copy(acc, dens_hbm, out_sems.at[PAIR_DEV])
    dens_out.start()

    loads[5].wait()
    arrived(1)

    @pl.loop(0, PAIR_DEV)
    def _(p):
        exch[p] += exchange_term(1, p)

    loads[6].wait()
    arrived(2)

    @pl.loop(0, PAIR_DEV)
    def _(p):
        whole = exch[p] + exchange_term(2, p)
        main, tail = amp_of(1, p)
        new[p] = (base_ref[p] - scale_ref[p] * whole).astype(BF16)
        energy = jnp.sum(whole[:, :MAIN] * main.astype(F32)) + jnp.sum(whole[:, MAIN:] * tail)
        energy_ref[p] = energy / npao
        pltpu.make_async_copy(new.at[p], new_hbm.at[p], out_sems.at[p]).start()

    for p in range(PAIR_DEV):
        pltpu.make_async_copy(new.at[p], new_hbm.at[p], out_sems.at[p]).wait()
    dens_out.wait()
    for n in range(3):
        sent(n)


def local(
    blocks, aux_domain, pao_domain, pao_gap, amplitudes, pair_partner, coupling_list, coupling_coef
):
    devices = lax.axis_size(("orb", "pair"))
    naux, npao = blocks.shape[1:]
    norb = aux_domain.shape[0]
    hbm = pl.BlockSpec(memory_space=pltpu.MemorySpace.HBM)
    smem = pl.BlockSpec(memory_space=pltpu.MemorySpace.SMEM)
    sds = jax.ShapeDtypeStruct
    widths = [hi - lo for lo, hi in CUTS]
    new_amps, energies, densities = pl.pallas_call(
        functools.partial(kernel, devices),
        out_shape=[
            sds((PAIR_DEV, npao, npao), BF16),
            sds((PAIR_DEV,), F32),
            sds((OCC_DEV, npao, npao), F32),
        ],
        in_specs=[smem] * 3 + [hbm] * 5,
        out_specs=[hbm, smem, hbm],
        scratch_shapes=[
            pltpu.VMEM((OCC_DEV, npao, naux), BF16),
            pltpu.VMEM((24, naux), jnp.int32),
            pltpu.VMEM((npao, norb), jnp.int32),
            pltpu.VMEM((npao, norb), F32),
            pltpu.VMEM((PAIR_DEV, npao, npao), BF16),
            pltpu.VMEM((norb, 3 * LANE), jnp.int32),
            pltpu.VMEM((norb, 3 * LANE), F32),
            pltpu.VMEM((3, OCC_DEV, npao, 2 * npao), BF16),
            pltpu.VMEM((PAIR_DEV, npao, naux), BF16),
            *[pltpu.VMEM((3, OCC_DEV, npao, w), BF16) for w in widths],
            pltpu.VMEM((PAIR_DEV, npao, npao), F32),
            pltpu.VMEM((PAIR_DEV, npao, npao), F32),
            pltpu.VMEM((PAIR_DEV, npao, npao), F32),
            pltpu.VMEM((npao, NCPL * npao), BF16),
            pltpu.VMEM((npao, NCPL * npao), BF16),
            pltpu.VMEM((OCC_DEV, npao, npao), F32),
            pltpu.VMEM((PAIR_DEV, npao, npao), BF16),
            pltpu.SemaphoreType.DMA((10,)),
            pltpu.SemaphoreType.DMA((4, 2)),
            pltpu.SemaphoreType.DMA((4, 2)),
            pltpu.SemaphoreType.DMA((PAIR_DEV + 1,)),
        ],
        compiler_params=pltpu.CompilerParams(
            collective_id=0, has_side_effects=True, vmem_limit_bytes=60 * 1024 * 1024
        ),
        name="update",
    )(
        pair_partner,
        coupling_list.T,
        coupling_coef.T,
        jnp.swapaxes(blocks, 1, 2),
        aux_domain,
        pao_domain.T,
        pao_gap.T,
        amplitudes,
    )
    return (new_amps, energies, densities)


def solution(mesh):
    return jax.shard_map(
        local,
        mesh=mesh,
        in_specs=(
            P(("orb", "pair"), None, None),
            P(),
            P(),
            P(),
            P(("orb", "pair"), None, None),
            P(),
            P(("orb", "pair"), None),
            P(("orb", "pair"), None),
        ),
        out_specs=(
            P(("orb", "pair"), None, None),
            P(("orb", "pair")),
            P(("orb", "pair"), None, None),
        ),
        check_vma=False,
    )
```

```python
import functools

import jax
import jax.numpy as jnp
from jax import lax
from jax.experimental import pallas as pl
from jax.experimental.pallas import tpu as pltpu
from jax.sharding import PartitionSpec as P

OCC_DEV = 4
PAIR_DEV = 8
NCPL = 4
F32 = jnp.float32
BF16 = jnp.bfloat16
MAIN = 256
LANE = 128
MESH = pl.DeviceIdType.MESH
CONTRACT_LAST = (((1,), (1,)), ((), ()))
CONTRACT_FIRST = (((0,), (0,)), ((), ()))
AMPS = OCC_DEV
BACK = OCC_DEV + 1


def column(row, rows):
    wide = jnp.broadcast_to(row, (LANE, row.shape[1]))
    return wide.T[:rows]


def wanted(row):
    return jnp.where(row < 0, -2, row)


def lanes(col, row):
    pieces = [
        jnp.where(col == row[:, at : at + LANE], F32(1), F32(0)).astype(BF16)
        for at in range(0, row.shape[1], LANE)
    ]
    return pieces[0] if len(pieces) == 1 else jnp.concatenate(pieces, axis=1)


def wrapped(index, length):
    return lax.rem(lax.rem(index, length) + length, length)


def dot(a, b, dims=(((1,), (0,)), ((), ()))):
    return lax.dot_general(a, b, dims, preferred_element_type=F32)


def kernel(
    devices,
    partner,
    near,
    coef,
    blocks_hbm,
    aux_hbm,
    pao_hbm,
    gap_hbm,
    amps_hbm,
    new,
    energy_ref,
    acc,
    own,
    aux,
    pao_window,
    gap_window,
    raw,
    tab,
    gap,
    amps,
    picked,
    turned,
    blocks,
    result_out,
    result_in,
    scale_ref,
    base_ref,
    rows_ref,
    cols_ref,
    local_sems,
    send_sems,
    recv_sems,
):
    pairs_axis = lax.axis_size("pair")
    me = lax.axis_index("orb") * pairs_axis + lax.axis_index("pair")
    npao, naux = own.shape[1:]
    norb = aux_hbm.shape[0]
    rest = npao - MAIN
    has = (me > 0, me < devices - 1)
    spot = lax.rem(me, 2 * pairs_axis)
    keeps = (
        jnp.logical_and(has[0], spot >= pairs_axis),
        jnp.logical_and(
            has[1], jnp.logical_or(spot < pairs_axis - 1, spot == 2 * pairs_axis - 1)
        ),
    )
    gives = tuple(jnp.logical_and(h, jnp.logical_not(k)) for h, k in zip(has, keeps))
    peers = tuple(
        (lax.div(at, pairs_axis), lax.rem(at, pairs_axis))
        for at in (lax.rem(me + devices - 1, devices), lax.rem(me + 1, devices))
    )

    groups = norb // 8
    group = me // 2
    aux_start = (group - 1) * 8
    loads = [
        pltpu.make_async_copy(src, dst, local_sems.at[n])
        for n, (src, dst) in enumerate(
            (
                (pao_hbm, pao_window),
                (amps_hbm, raw),
                (blocks_hbm, own),
                (gap_hbm, gap_window),
                (blocks_hbm, blocks.at[1]),
                *[
                    (
                        aux_hbm.at[pl.ds(lax.rem(group + groups - 1 + g, groups) * 8, 8)],
                        aux.at[8 * g : 8 * g + 8],
                    )
                    for g in range(3)
                ],
            )
        )
    ]
    for copy in loads:
        copy.start()

    barrier = pltpu.get_barrier_semaphore()
    for side in range(2):

        @pl.when(has[side])
        def _(side=side):
            pl.semaphore_signal(barrier, inc=1, device_id=peers[side], device_id_type=MESH)

    inner = jnp.logical_and(*has)

    @pl.when(inner)
    def _():
        pl.semaphore_wait(barrier, 2)

    @pl.when(jnp.logical_not(inner))
    def _():
        pl.semaphore_wait(barrier, 1)

    def remote(n, side, back):
        if not back and isinstance(n, int) and n == AMPS:
            src, dst = amps.at[1], amps.at[2 - 2 * side]
        elif back:
            src, dst = result_out.at[side, n - BACK], result_in.at[1 - side, n - BACK]
        else:
            src, dst = blocks_hbm.at[n], blocks.at[2 - 2 * side, n]
        return pltpu.make_async_remote_copy(
            src_ref=src,
            dst_ref=dst,
            send_sem=send_sems.at[n, side],
            recv_sem=recv_sems.at[n, side],
            device_id=peers[side],
            device_id_type=MESH,
        )

    def each(senders, act, back=False):
        for side in range(2):

            @pl.when(senders[side])
            def _(side=side):
                act(side, back)

    def start(n, senders, back=False):
        each(senders, lambda side, back: remote(n, side, back).start(), back)

    def sent(n, senders, back=False):
        each(senders, lambda side, back: remote(n, side, back).wait_send(), back)

    def arrived(n, receivers, back=False):
        each(receivers, lambda side, back: remote(n, 1 - side, back).wait_recv(), back)

    start(0, gives)

    def rows_of(window):
        x = window[...]
        return jnp.concatenate([x, x[MAIN:]], axis=0).T

    loads[0].wait()
    tab[...] = rows_of(pao_window)
    loads[1].wait()
    first = me * OCC_DEV

    @pl.loop(0, OCC_DEV)
    def _(k):
        left = column(tab[pl.ds(first + k, 1), :], npao)[:, :1] >= 0
        tails = []
        for n in range(2):
            p = k + n * OCC_DEV
            at = partner[me * PAIR_DEV + p]
            keep = left & (tab[pl.ds(at, 1), :] >= 0)[:, :npao]
            amp = jnp.where(keep, raw[p].astype(F32), F32(0))
            amps[1, k, :, n * MAIN : (n + 1) * MAIN] = amp[:, :MAIN].astype(BF16)
            tails.append(amp[:, MAIN:])
        amps[1, k, :, 2 * MAIN :] = jnp.concatenate(tails, axis=1).astype(BF16)

    loads[3].wait()
    gap[...] = rows_of(gap_window)
    for side in range(2):

        @pl.when(jnp.logical_not(has[side]))
        def _(side=side):
            amps[2 * side] = jnp.zeros_like(amps[2 * side])

    loads[2].wait()
    for g in range(3):
        loads[5 + g].wait()

    def aligned(out, o, other):
        col = column(aux[pl.ds(me * OCC_DEV + o - aux_start, 1), :], naux)
        present = aux[pl.ds(other, 1), :]
        for at in range(0, naux, MAIN):
            pick = lanes(col, present[:, at : at + MAIN])
            out[:, at : at + MAIN] = dot(own[o], pick).astype(BF16)

    def align(p):
        second = wrapped(partner[me * PAIR_DEV + p] - aux_start, aux.shape[0])
        aligned(picked.at[p], lax.rem(p, OCC_DEV), second)

    pl.loop(0, 1)(align)
    start(AMPS, has)
    for side in range(2):

        @pl.when(keeps[side])
        def _(side=side):
            far = me - 1 + 2 * side

            @pl.loop(0, PAIR_DEV)
            def _(p):
                o = wrapped(partner[far * PAIR_DEV + p] - me * OCC_DEV, OCC_DEV)
                first = far * OCC_DEV + lax.rem(p, OCC_DEV) - aux_start
                aligned(turned.at[side, p], o, first)

    pl.loop(1, PAIR_DEV // 2)(align)
    busy = jnp.logical_and(*keeps)

    @pl.when(jnp.logical_not(busy))
    def _():
        pl.loop(PAIR_DEV // 2, PAIR_DEV)(align)

    def exchange_back(k):
        for side in range(2):

            @pl.when(keeps[side])
            def _(side=side):
                tails = []
                for n in range(2):
                    whole = dot(blocks[2 * side, k], turned[side, k + n * OCC_DEV], CONTRACT_LAST)
                    result_out[side, k, :, n * MAIN : (n + 1) * MAIN] = whole[:, :MAIN].astype(BF16)
                    tails.append(whole[:, MAIN:])
                result_out[side, k, :, 2 * MAIN :] = jnp.concatenate(tails, axis=1).astype(BF16)

    def amp_of(side, p):
        k, half = lax.rem(p, OCC_DEV), lax.div(p, OCC_DEV)
        main = amps[side, k, :, pl.ds(pl.multiple_of(half * MAIN, MAIN), MAIN)]
        tail = amps[side, k, :, 2 * MAIN :].astype(F32)
        tail = jnp.where(half == 0, tail, pltpu.roll(tail, rest, 1))
        return main, tail[:, :rest]

    def right_terms(side):
        @pl.loop(0, PAIR_DEV)
        def _(p):
            q = lax.rem((me + devices - 1 + side) * PAIR_DEV + p, devices * PAIR_DEV)
            target = partner[q] - me * OCC_DEV
            main, tail = amp_of(side, p)
            whole = jnp.concatenate([main, tail.astype(BF16)], axis=1)
            term = dot(whole, whole, CONTRACT_FIRST)
            for o in range(OCC_DEV):
                acc[o] += jnp.where(target == o, F32(1), F32(0)) * term

    for o in range(OCC_DEV):
        packed = amps[1, o]
        acc[o] = dot(packed, packed, CONTRACT_LAST)
    right_terms(1)

    arrived(0, keeps)
    exchange_back(0)
    sent(AMPS, has)
    start(1, gives)
    start(2, gives)
    arrived(AMPS, has)
    low = lax.broadcasted_iota(jnp.int32, (1, 2 * rest), 1) < rest

    def couple(p):
        i_row = me * OCC_DEV + lax.rem(p, OCC_DEV)
        j_row = partner[me * PAIR_DEV + p]
        left = column(wanted(tab[pl.ds(i_row, 1), :]), npao)
        right = column(wanted(tab[pl.ds(j_row, 1), :]), npao)
        held_rest, held_row = None, None
        for c in range(NCPL):
            m = near[c, p]
            spot = wrapped(m - (me - 1) * PAIR_DEV, 3 * PAIR_DEV)
            side, inner = lax.div(spot, PAIR_DEV), lax.rem(spot, PAIR_DEV)
            slot, half = lax.rem(inner, OCC_DEV), lax.div(inner, OCC_DEV)
            i_m = lax.div(m, PAIR_DEV) * OCC_DEV + slot
            j_m = partner[m]
            scale = coef[c, p]
            pick = lanes(left, tab[pl.ds(i_m, 1), :])[:, :npao]
            both = amps[side, slot]
            main = jnp.where(half == 0, both[:, :MAIN], both[:, MAIN : 2 * MAIN])
            tail = both[:, 2 * MAIN :]
            rows_ref[:, c * MAIN : (c + 1) * MAIN] = (dot(pick, main) * scale).astype(BF16)
            got = dot(pick, tail) * scale
            got = jnp.where(half == c % 2, got, pltpu.roll(got, rest, 1))
            row = tab[pl.ds(j_m, 1), :]
            cols_ref[:, c * MAIN : (c + 1) * MAIN] = lanes(right, row[:, :MAIN])
            row = row[:, MAIN:]
            if c % 2 == 0:
                held_rest, held_row = got, row
            else:
                at = NCPL * MAIN + (c // 2) * 2 * rest
                rows_ref[:, at : at + 2 * rest] = jnp.where(low, held_rest, got).astype(BF16)
                cols_ref[:, at : at + 2 * rest] = lanes(right, jnp.where(low, held_row, row))
        coupling = dot(rows_ref[...], cols_ref[...], CONTRACT_LAST)
        gap_left = column(gap[pl.ds(i_row, 1), :], npao)[:, :1]
        gap_right = gap[pl.ds(j_row, 1), :]
        keep_right = tab[pl.ds(j_row, 1), :] >= 0
        main, tail = amp_of(1, p)
        for lo, hi, amp in ((0, MAIN, main.astype(F32)), (MAIN, npao, tail)):
            keep = (left[:, :1] >= 0) & keep_right[:, lo:hi]
            denom = gap_left + gap_right[:, lo:hi]
            half_inverse = 0.5 / denom
            scale_ref[p, :, lo:hi] = jnp.where(keep, half_inverse, F32(0))
            base_ref[p, :, lo:hi] = amp - (denom * amp - coupling[:, lo:hi]) * half_inverse

    pl.loop(0, 1)(couple)
    start(BACK, keeps, True)
    pl.loop(1, 4)(couple)
    sent(1, gives)
    start(3, gives)
    pl.loop(4, 5)(couple)
    arrived(1, keeps)
    exchange_back(1)
    pl.loop(5, 6)(couple)
    start(BACK + 1, keeps, True)
    arrived(2, keeps)
    exchange_back(2)
    pl.loop(6, 7)(couple)
    start(BACK + 2, keeps, True)
    pl.loop(7, 8)(couple)
    right_terms(0)
    right_terms(2)
    loads[4].wait()
    arrived(3, keeps)
    exchange_back(3)

    def finish(k):
        arrived(BACK + k, gives, True)
        for n in range(2):
            p = k + n * OCC_DEV
            spot = wrapped(partner[me * PAIR_DEV + p] - (me - 1) * OCC_DEV, 3 * OCC_DEV)
            side, slot = lax.div(spot, OCC_DEV), lax.rem(spot, OCC_DEV)
            whole = dot(picked[p], blocks[side, slot], CONTRACT_LAST)
            amp = amps[1, k]
            tail = amp[:, 2 * MAIN + n * rest : 2 * MAIN + (n + 1) * rest].astype(F32)
            energy = F32(0)
            for lo, hi, at, value in (
                (0, MAIN, n * MAIN, amp[:, n * MAIN : (n + 1) * MAIN].astype(F32)),
                (MAIN, npao, 2 * MAIN + n * rest, tail),
            ):
                exchange = whole[:, lo:hi]
                for far in range(2):
                    came = jnp.logical_and(gives[far], side == 2 * far)
                    other = result_in[far, k, :, at : at + hi - lo].astype(F32)
                    exchange = jnp.where(came, other, exchange)
                new[p, :, lo:hi] = (
                    base_ref[p, :, lo:hi] - scale_ref[p, :, lo:hi] * exchange
                ).astype(BF16)
                energy += jnp.sum(exchange * value)
            energy_ref[p] = energy / npao

    @pl.when(busy)
    def _():
        pl.loop(PAIR_DEV // 2, PAIR_DEV // 2 + 1)(align)

    acc[...] = acc[...] / npao
    start(BACK + 3, keeps, True)

    @pl.when(busy)
    def _():
        pl.loop(PAIR_DEV // 2 + 1, PAIR_DEV)(align)

    pl.loop(0, 1)(finish)
    pl.loop(1, OCC_DEV)(finish)
    sent(0, gives)
    sent(2, gives)
    sent(3, gives)
    for k in range(OCC_DEV):
        sent(BACK + k, keeps, True)


def local(
    blocks, aux_domain, pao_domain, pao_gap, amplitudes, pair_partner, coupling_list, coupling_coef
):
    devices = lax.axis_size(("orb", "pair"))
    naux, npao = blocks.shape[1:]
    norb = aux_domain.shape[0]
    hbm = pl.BlockSpec(memory_space=pltpu.MemorySpace.HBM)
    smem = pl.BlockSpec(memory_space=pltpu.MemorySpace.SMEM)
    vmem = pl.BlockSpec(memory_space=pltpu.MemorySpace.VMEM)
    sds = jax.ShapeDtypeStruct
    new_amps, energies, densities = pl.pallas_call(
        functools.partial(kernel, devices),
        out_shape=[
            pltpu.VMEM((PAIR_DEV, npao, npao), BF16),
            sds((PAIR_DEV,), F32),
            pltpu.VMEM((OCC_DEV, npao, npao), F32),
        ],
        in_specs=[smem] * 3 + [hbm] * 5,
        out_specs=[vmem, smem, vmem],
        scratch_shapes=[
            pltpu.VMEM((OCC_DEV, npao, naux), BF16),
            pltpu.VMEM((24, naux), jnp.int32),
            pltpu.VMEM((npao, norb), jnp.int32),
            pltpu.VMEM((npao, norb), F32),
            pltpu.VMEM((PAIR_DEV, npao, npao), BF16),
            pltpu.VMEM((norb, 3 * LANE), jnp.int32),
            pltpu.VMEM((norb, 3 * LANE), F32),
            pltpu.VMEM((3, OCC_DEV, npao, 2 * npao), BF16),
            pltpu.VMEM((PAIR_DEV, npao, naux), BF16),
            pltpu.VMEM((2, PAIR_DEV, npao, naux), BF16),
            pltpu.VMEM((3, OCC_DEV, npao, naux), BF16),
            pltpu.VMEM((2, OCC_DEV, npao, 2 * npao), BF16),
            pltpu.VMEM((2, OCC_DEV, npao, 2 * npao), BF16),
            pltpu.VMEM((PAIR_DEV, npao, npao), F32),
            pltpu.VMEM((PAIR_DEV, npao, npao), F32),
            pltpu.VMEM((npao, NCPL * npao), BF16),
            pltpu.VMEM((npao, NCPL * npao), BF16),
            pltpu.SemaphoreType.DMA((8,)),
            pltpu.SemaphoreType.DMA((2 * OCC_DEV + 1, 2)),
            pltpu.SemaphoreType.DMA((2 * OCC_DEV + 1, 2)),
        ],
        compiler_params=pltpu.CompilerParams(
            collective_id=0, has_side_effects=True, vmem_limit_bytes=60 * 1024 * 1024
        ),
        name="update",
    )(
        pair_partner,
        coupling_list.T,
        coupling_coef.T,
        jnp.swapaxes(blocks, 1, 2),
        aux_domain,
        pao_domain.T,
        pao_gap.T,
        amplitudes,
    )
    return (new_amps, energies, densities)


def solution(mesh):
    return jax.shard_map(
        local,
        mesh=mesh,
        in_specs=(
            P(("orb", "pair"), None, None),
            P(),
            P(),
            P(),
            P(("orb", "pair"), None, None),
            P(),
            P(("orb", "pair"), None),
            P(("orb", "pair"), None),
        ),
        out_specs=(
            P(("orb", "pair"), None, None),
            P(("orb", "pair")),
            P(("orb", "pair"), None, None),
        ),
        check_vma=False,
    )
```

```python
import functools

import jax
import jax.numpy as jnp
from jax import lax
from jax.experimental import pallas as pl
from jax.experimental.pallas import tpu as pltpu
from jax.sharding import PartitionSpec as P

OCC_DEV = 4
PAIR_DEV = 8
NCPL = 4
F32 = jnp.float32
BF16 = jnp.bfloat16
MAIN = 256
LANE = 128
MESH = pl.DeviceIdType.MESH
CONTRACT_LAST = (((1,), (1,)), ((), ()))
CONTRACT_FIRST = (((0,), (0,)), ((), ()))
AMPS = OCC_DEV
BACK = OCC_DEV + 1
LAST = OCC_DEV - 1
LAST_LOW = BACK + OCC_DEV
LAST_BACK_LOW = LAST_LOW + 1


def column(row, rows):
    wide = jnp.broadcast_to(row, (LANE, row.shape[1]))
    return wide.T[:rows]


def wanted(row):
    return jnp.where(row < 0, -2, row)


def lanes(col, row):
    pieces = [
        jnp.where(col == row[:, at : at + LANE], F32(1), F32(0)).astype(BF16)
        for at in range(0, row.shape[1], LANE)
    ]
    return pieces[0] if len(pieces) == 1 else jnp.concatenate(pieces, axis=1)


def wrapped(index, length):
    return lax.rem(lax.rem(index, length) + length, length)


def dot(a, b, dims=(((1,), (0,)), ((), ()))):
    return lax.dot_general(a, b, dims, preferred_element_type=F32)


def kernel(
    devices,
    partner,
    near,
    coef,
    blocks_hbm,
    aux_hbm,
    pao_hbm,
    gap_hbm,
    amps_hbm,
    new,
    energy_ref,
    acc,
    own,
    aux,
    pao_window,
    gap_window,
    raw,
    tab,
    gap,
    amps,
    picked,
    turned,
    blocks,
    result_out,
    result_in,
    scale_ref,
    base_ref,
    rows_ref,
    cols_ref,
    local_sems,
    send_sems,
    recv_sems,
):
    pairs_axis = lax.axis_size("pair")
    me = lax.axis_index("orb") * pairs_axis + lax.axis_index("pair")
    npao, naux = own.shape[1:]
    norb = aux_hbm.shape[0]
    rest = npao - MAIN
    has = (me > 0, me < devices - 1)
    spot = lax.rem(me, 2 * pairs_axis)
    keeps = (
        jnp.logical_and(has[0], spot >= pairs_axis),
        jnp.logical_and(
            has[1], jnp.logical_or(spot < pairs_axis - 1, spot == 2 * pairs_axis - 1)
        ),
    )
    gives = tuple(jnp.logical_and(h, jnp.logical_not(k)) for h, k in zip(has, keeps))
    peers = tuple(
        (lax.div(at, pairs_axis), lax.rem(at, pairs_axis))
        for at in (lax.rem(me + devices - 1, devices), lax.rem(me + 1, devices))
    )

    groups = norb // 8
    group = me // 2
    aux_start = (group - 1) * 8
    loads = [
        pltpu.make_async_copy(src, dst, local_sems.at[n])
        for n, (src, dst) in enumerate(
            (
                (pao_hbm, pao_window),
                (amps_hbm, raw),
                (blocks_hbm, own),
                (gap_hbm, gap_window),
                (blocks_hbm, blocks.at[1]),
                *[
                    (
                        aux_hbm.at[pl.ds(lax.rem(group + groups - 1 + g, groups) * 8, 8)],
                        aux.at[8 * g : 8 * g + 8],
                    )
                    for g in range(3)
                ],
            )
        )
    ]
    for copy in loads:
        copy.start()

    barrier = pltpu.get_barrier_semaphore()
    for side in range(2):

        @pl.when(has[side])
        def _(side=side):
            pl.semaphore_signal(barrier, inc=1, device_id=peers[side], device_id_type=MESH)

    inner = jnp.logical_and(*has)

    @pl.when(inner)
    def _():
        pl.semaphore_wait(barrier, 2)

    @pl.when(jnp.logical_not(inner))
    def _():
        pl.semaphore_wait(barrier, 1)

    def remote(n, side, back):
        number = n if isinstance(n, int) else -1
        half = npao // 2
        if number == AMPS:
            src, dst = amps.at[1], amps.at[2 - 2 * side]
        elif number in (BACK + LAST, LAST_BACK_LOW):
            rows = slice(0, half) if number == BACK + LAST else slice(half, npao)
            src, dst = result_out.at[side, LAST, rows], result_in.at[1 - side, LAST, rows]
        elif number in (LAST, LAST_LOW):
            rows = slice(0, half) if number == LAST else slice(half, npao)
            src, dst = blocks_hbm.at[LAST, rows], blocks.at[2 - 2 * side, LAST, rows]
        elif back:
            src, dst = result_out.at[side, n - BACK], result_in.at[1 - side, n - BACK]
        else:
            src, dst = blocks_hbm.at[n], blocks.at[2 - 2 * side, n]
        return pltpu.make_async_remote_copy(
            src_ref=src,
            dst_ref=dst,
            send_sem=send_sems.at[n, side],
            recv_sem=recv_sems.at[n, side],
            device_id=peers[side],
            device_id_type=MESH,
        )

    def each(senders, act, back=False):
        for side in range(2):

            @pl.when(senders[side])
            def _(side=side):
                act(side, back)

    def start(n, senders, back=False):
        each(senders, lambda side, back: remote(n, side, back).start(), back)

    def sent(n, senders, back=False):
        each(senders, lambda side, back: remote(n, side, back).wait_send(), back)

    def arrived(n, receivers, back=False):
        each(receivers, lambda side, back: remote(n, 1 - side, back).wait_recv(), back)

    start(0, gives)

    def rows_of(window):
        x = window[...]
        return jnp.concatenate([x, x[MAIN:]], axis=0).T

    loads[0].wait()
    tab[...] = rows_of(pao_window)
    loads[1].wait()
    first = me * OCC_DEV

    @pl.loop(0, OCC_DEV)
    def _(k):
        left = column(tab[pl.ds(first + k, 1), :], npao)[:, :1] >= 0
        tails = []
        for n in range(2):
            p = k + n * OCC_DEV
            at = partner[me * PAIR_DEV + p]
            keep = left & (tab[pl.ds(at, 1), :] >= 0)[:, :npao]
            amp = jnp.where(keep, raw[p].astype(F32), F32(0))
            amps[1, k, :, n * MAIN : (n + 1) * MAIN] = amp[:, :MAIN].astype(BF16)
            tails.append(amp[:, MAIN:])
        amps[1, k, :, 2 * MAIN :] = jnp.concatenate(tails, axis=1).astype(BF16)

    loads[3].wait()
    gap[...] = rows_of(gap_window)
    for side in range(2):

        @pl.when(jnp.logical_not(has[side]))
        def _(side=side):
            amps[2 * side] = jnp.zeros_like(amps[2 * side])

    loads[2].wait()
    for g in range(3):
        loads[5 + g].wait()

    def aligned(out, o, other):
        col = column(aux[pl.ds(me * OCC_DEV + o - aux_start, 1), :], naux)
        present = aux[pl.ds(other, 1), :]
        for at in range(0, naux, MAIN):
            pick = lanes(col, present[:, at : at + MAIN])
            out[:, at : at + MAIN] = dot(own[o], pick).astype(BF16)

    def align(p):
        second = wrapped(partner[me * PAIR_DEV + p] - aux_start, aux.shape[0])
        aligned(picked.at[p], lax.rem(p, OCC_DEV), second)

    pl.loop(0, 1)(align)
    start(AMPS, has)
    for side in range(2):

        @pl.when(keeps[side])
        def _(side=side):
            far = me - 1 + 2 * side

            @pl.loop(0, PAIR_DEV)
            def _(p):
                o = wrapped(partner[far * PAIR_DEV + p] - me * OCC_DEV, OCC_DEV)
                first = far * OCC_DEV + lax.rem(p, OCC_DEV) - aux_start
                aligned(turned.at[side, p], o, first)

    pl.loop(1, PAIR_DEV // 2)(align)
    busy = jnp.logical_and(*keeps)

    @pl.when(jnp.logical_not(busy))
    def _():
        pl.loop(PAIR_DEV // 2, PAIR_DEV)(align)

    def exchange_back(k, lo=0, hi=npao):
        for side in range(2):

            @pl.when(keeps[side])
            def _(side=side):
                tails = []
                for n in range(2):
                    whole = dot(
                        blocks[2 * side, k, lo:hi], turned[side, k + n * OCC_DEV], CONTRACT_LAST
                    )
                    at = slice(n * MAIN, (n + 1) * MAIN)
                    result_out[side, k, lo:hi, at] = whole[:, :MAIN].astype(BF16)
                    tails.append(whole[:, MAIN:])
                result_out[side, k, lo:hi, 2 * MAIN :] = jnp.concatenate(tails, axis=1).astype(BF16)

    def amp_of(side, p):
        k, half = lax.rem(p, OCC_DEV), lax.div(p, OCC_DEV)
        main = amps[side, k, :, pl.ds(pl.multiple_of(half * MAIN, MAIN), MAIN)]
        tail = amps[side, k, :, 2 * MAIN :].astype(F32)
        tail = jnp.where(half == 0, tail, pltpu.roll(tail, rest, 1))
        return main, tail[:, :rest]

    def right_terms(side, first=0, last=PAIR_DEV):
        @pl.loop(first, last)
        def _(p):
            q = lax.rem((me + devices - 1 + side) * PAIR_DEV + p, devices * PAIR_DEV)
            target = partner[q] - me * OCC_DEV
            main, tail = amp_of(side, p)
            whole = jnp.concatenate([main, tail.astype(BF16)], axis=1)
            term = dot(whole, whole, CONTRACT_FIRST)
            for o in range(OCC_DEV):
                acc[o] += jnp.where(target == o, F32(1), F32(0)) * term

    for o in range(OCC_DEV):
        packed = amps[1, o]
        acc[o] = dot(packed, packed, CONTRACT_LAST)
    right_terms(1)

    arrived(0, keeps)
    exchange_back(0)
    sent(AMPS, has)
    start(1, gives)
    start(2, gives)
    arrived(AMPS, has)
    low = lax.broadcasted_iota(jnp.int32, (1, 2 * rest), 1) < rest

    def couple(p):
        i_row = me * OCC_DEV + lax.rem(p, OCC_DEV)
        j_row = partner[me * PAIR_DEV + p]
        left = column(wanted(tab[pl.ds(i_row, 1), :]), npao)
        right = column(wanted(tab[pl.ds(j_row, 1), :]), npao)
        held_rest, held_row = None, None
        for c in range(NCPL):
            m = near[c, p]
            spot = wrapped(m - (me - 1) * PAIR_DEV, 3 * PAIR_DEV)
            side, inner = lax.div(spot, PAIR_DEV), lax.rem(spot, PAIR_DEV)
            slot, half = lax.rem(inner, OCC_DEV), lax.div(inner, OCC_DEV)
            i_m = lax.div(m, PAIR_DEV) * OCC_DEV + slot
            j_m = partner[m]
            scale = coef[c, p]
            pick = lanes(left, tab[pl.ds(i_m, 1), :])[:, :npao]
            both = amps[side, slot]
            main = jnp.where(half == 0, both[:, :MAIN], both[:, MAIN : 2 * MAIN])
            tail = both[:, 2 * MAIN :]
            rows_ref[:, c * MAIN : (c + 1) * MAIN] = (dot(pick, main) * scale).astype(BF16)
            got = dot(pick, tail) * scale
            got = jnp.where(half == c % 2, got, pltpu.roll(got, rest, 1))
            row = tab[pl.ds(j_m, 1), :]
            cols_ref[:, c * MAIN : (c + 1) * MAIN] = lanes(right, row[:, :MAIN])
            row = row[:, MAIN:]
            if c % 2 == 0:
                held_rest, held_row = got, row
            else:
                at = NCPL * MAIN + (c // 2) * 2 * rest
                rows_ref[:, at : at + 2 * rest] = jnp.where(low, held_rest, got).astype(BF16)
                cols_ref[:, at : at + 2 * rest] = lanes(right, jnp.where(low, held_row, row))
        coupling = dot(rows_ref[...], cols_ref[...], CONTRACT_LAST)
        gap_left = column(gap[pl.ds(i_row, 1), :], npao)[:, :1]
        gap_right = gap[pl.ds(j_row, 1), :]
        keep_right = tab[pl.ds(j_row, 1), :] >= 0
        main, tail = amp_of(1, p)
        for lo, hi, amp in ((0, MAIN, main.astype(F32)), (MAIN, npao, tail)):
            keep = (left[:, :1] >= 0) & keep_right[:, lo:hi]
            denom = gap_left + gap_right[:, lo:hi]
            half_inverse = 0.5 / denom
            scale_ref[p, :, lo:hi] = jnp.where(keep, half_inverse, F32(0))
            base_ref[p, :, lo:hi] = amp - (denom * amp - coupling[:, lo:hi]) * half_inverse

    pl.loop(0, 1)(couple)
    start(BACK, keeps, True)
    pl.loop(1, 4)(couple)
    sent(1, gives)
    start(3, gives)
    pl.loop(4, 5)(couple)
    arrived(1, keeps)
    exchange_back(1)
    pl.loop(5, 6)(couple)
    start(BACK + 1, keeps, True)
    arrived(2, keeps)
    exchange_back(2)
    pl.loop(6, 7)(couple)
    start(BACK + 2, keeps, True)
    sent(2, gives)
    start(LAST_LOW, gives)
    pl.loop(7, 8)(couple)
    right_terms(0)
    loads[4].wait()
    arrived(LAST, keeps)
    exchange_back(LAST, 0, npao // 2)
    right_terms(2, 0, 2)
    start(BACK + LAST, keeps, True)
    right_terms(2, 2, PAIR_DEV)
    acc[...] = acc[...] / npao

    def finish(k, parts=(0, 1)):
        for n in parts:
            p = k + n * OCC_DEV
            spot = wrapped(partner[me * PAIR_DEV + p] - (me - 1) * OCC_DEV, 3 * OCC_DEV)
            side, slot = lax.div(spot, OCC_DEV), lax.rem(spot, OCC_DEV)
            whole = dot(picked[p], blocks[side, slot], CONTRACT_LAST)
            amp = amps[1, k]
            tail = amp[:, 2 * MAIN + n * rest : 2 * MAIN + (n + 1) * rest].astype(F32)
            energy = F32(0)
            for lo, hi, at, value in (
                (0, MAIN, n * MAIN, amp[:, n * MAIN : (n + 1) * MAIN].astype(F32)),
                (MAIN, npao, 2 * MAIN + n * rest, tail),
            ):
                exchange = whole[:, lo:hi]
                for far in range(2):
                    came = jnp.logical_and(gives[far], side == 2 * far)
                    other = result_in[far, k, :, at : at + hi - lo].astype(F32)
                    exchange = jnp.where(came, other, exchange)
                new[p, :, lo:hi] = (
                    base_ref[p, :, lo:hi] - scale_ref[p, :, lo:hi] * exchange
                ).astype(BF16)
                energy += jnp.sum(exchange * value)
            energy_ref[pl.ds(p, 1), :] = jnp.full((1, LANE), energy / npao, F32)

    for k in range(LAST):
        arrived(BACK + k, gives, True)

    arrived(LAST_LOW, keeps)
    exchange_back(LAST, npao // 2, npao)
    pl.loop(0, 1)(lambda k: finish(k, (0,)))
    start(LAST_BACK_LOW, keeps, True)

    @pl.when(busy)
    def _():
        pl.loop(PAIR_DEV // 2, PAIR_DEV)(align)

    pl.loop(0, 1)(lambda k: finish(k, (1,)))
    pl.loop(1, LAST)(finish)
    arrived(BACK + LAST, gives, True)
    arrived(LAST_BACK_LOW, gives, True)
    pl.loop(LAST, OCC_DEV)(finish)
    sent(0, gives)
    sent(LAST, gives)
    sent(LAST_LOW, gives)
    for k in range(OCC_DEV):
        sent(BACK + k, keeps, True)
    sent(LAST_BACK_LOW, keeps, True)


def write_kernel(new, energy, dens, new_hbm, energy_out, dens_hbm, sems):
    half = new.shape[1] // 2
    pieces = [(new, new_hbm, p) for p in range(PAIR_DEV)]
    pieces += [(dens, dens_hbm, o) for o in range(OCC_DEV)]
    copies = [
        pltpu.make_async_copy(
            src.at[n, part * half : (part + 1) * half],
            dst.at[n, part * half : (part + 1) * half],
            sems.at[2 * at + part],
        )
        for at, (src, dst, n) in enumerate(pieces)
        for part in range(2)
    ]
    for copy in copies:
        copy.start()
    for p in range(PAIR_DEV):
        energy_out[p] = energy[p, 0]
    for copy in copies:
        copy.wait()


def local(
    blocks, aux_domain, pao_domain, pao_gap, amplitudes, pair_partner, coupling_list, coupling_coef
):
    devices = lax.axis_size(("orb", "pair"))
    naux, npao = blocks.shape[1:]
    norb = aux_domain.shape[0]
    hbm = pl.BlockSpec(memory_space=pltpu.MemorySpace.HBM)
    smem = pl.BlockSpec(memory_space=pltpu.MemorySpace.SMEM)
    vmem = pl.BlockSpec(memory_space=pltpu.MemorySpace.VMEM)
    sds = jax.ShapeDtypeStruct
    new_amps, energies, densities = pl.pallas_call(
        functools.partial(kernel, devices),
        out_shape=[
            pltpu.VMEM((PAIR_DEV, npao, npao), BF16),
            pltpu.VMEM((PAIR_DEV, LANE), F32),
            pltpu.VMEM((OCC_DEV, npao, npao), F32),
        ],
        in_specs=[smem] * 3 + [hbm] * 5,
        out_specs=[vmem, vmem, vmem],
        scratch_shapes=[
            pltpu.VMEM((OCC_DEV, npao, naux), BF16),
            pltpu.VMEM((24, naux), jnp.int32),
            pltpu.VMEM((npao, norb), jnp.int32),
            pltpu.VMEM((npao, norb), F32),
            pltpu.VMEM((PAIR_DEV, npao, npao), BF16),
            pltpu.VMEM((norb, 3 * LANE), jnp.int32),
            pltpu.VMEM((norb, 3 * LANE), F32),
            pltpu.VMEM((3, OCC_DEV, npao, 2 * npao), BF16),
            pltpu.VMEM((PAIR_DEV, npao, naux), BF16),
            pltpu.VMEM((2, PAIR_DEV, npao, naux), BF16),
            pltpu.VMEM((3, OCC_DEV, npao, naux), BF16),
            pltpu.VMEM((2, OCC_DEV, npao, 2 * npao), BF16),
            pltpu.VMEM((2, OCC_DEV, npao, 2 * npao), BF16),
            pltpu.VMEM((PAIR_DEV, npao, npao), F32),
            pltpu.VMEM((PAIR_DEV, npao, npao), F32),
            pltpu.VMEM((npao, NCPL * npao), BF16),
            pltpu.VMEM((npao, NCPL * npao), BF16),
            pltpu.SemaphoreType.DMA((8,)),
            pltpu.SemaphoreType.DMA((LAST_BACK_LOW + 1, 2)),
            pltpu.SemaphoreType.DMA((LAST_BACK_LOW + 1, 2)),
        ],
        compiler_params=pltpu.CompilerParams(
            collective_id=0, has_side_effects=True, vmem_limit_bytes=60 * 1024 * 1024
        ),
        name="update",
    )(
        pair_partner,
        coupling_list.T,
        coupling_coef.T,
        jnp.swapaxes(blocks, 1, 2),
        aux_domain,
        pao_domain.T,
        pao_gap.T,
        amplitudes,
    )
    return pl.pallas_call(
        write_kernel,
        out_shape=[
            sds((PAIR_DEV, npao, npao), BF16),
            sds((PAIR_DEV,), F32),
            sds((OCC_DEV, npao, npao), F32),
        ],
        in_specs=[vmem, vmem, vmem],
        out_specs=[hbm, smem, hbm],
        scratch_shapes=[pltpu.SemaphoreType.DMA((2 * (PAIR_DEV + OCC_DEV),))],
        compiler_params=pltpu.CompilerParams(vmem_limit_bytes=1024 * 1024),
        name="write",
    )(new_amps, energies, densities)


def solution(mesh):
    return jax.shard_map(
        local,
        mesh=mesh,
        in_specs=(
            P(("orb", "pair"), None, None),
            P(),
            P(),
            P(),
            P(("orb", "pair"), None, None),
            P(),
            P(("orb", "pair"), None),
            P(("orb", "pair"), None),
        ),
        out_specs=(
            P(("orb", "pair"), None, None),
            P(("orb", "pair")),
            P(("orb", "pair"), None, None),
        ),
        check_vma=False,
    )
```

```python
import functools

import jax
import jax.numpy as jnp
from jax import lax
from jax.experimental import pallas as pl
from jax.experimental.pallas import tpu as pltpu
from jax.sharding import PartitionSpec as P

OCC_DEV = 4
PAIR_DEV = 8
NCPL = 4
F32 = jnp.float32
BF16 = jnp.bfloat16
MAIN = 256
LANE = 128
MESH = pl.DeviceIdType.MESH
CONTRACT_LAST = (((1,), (1,)), ((), ()))
CONTRACT_FIRST = (((0,), (0,)), ((), ()))
AMPS = OCC_DEV
BACK = OCC_DEV + 1
LAST = OCC_DEV - 1
LAST_LOW = BACK + OCC_DEV
LAST_BACK_LOW = LAST_LOW + 1


def column(row, rows):
    wide = jnp.broadcast_to(row, (LANE, row.shape[1]))
    return wide.T[:rows]


def wanted(row):
    return jnp.where(row < 0, -2, row)


def lanes(col, row):
    pieces = [
        jnp.where(col == row[:, at : at + LANE], F32(1), F32(0)).astype(BF16)
        for at in range(0, row.shape[1], LANE)
    ]
    return pieces[0] if len(pieces) == 1 else jnp.concatenate(pieces, axis=1)


def wrapped(index, length):
    return lax.rem(lax.rem(index, length) + length, length)


def dot(a, b, dims=(((1,), (0,)), ((), ()))):
    return lax.dot_general(a, b, dims, preferred_element_type=F32)


def kernel(
    devices,
    partner,
    near,
    coef,
    blocks_hbm,
    aux_hbm,
    pao_hbm,
    gap_hbm,
    amps_hbm,
    new,
    energy_ref,
    acc,
    own,
    aux,
    pao_window,
    gap_window,
    raw,
    tab,
    gap,
    amps,
    picked,
    turned,
    blocks,
    result_out,
    result_in,
    scale_ref,
    base_ref,
    rows_ref,
    cols_ref,
    local_sems,
    send_sems,
    recv_sems,
):
    pairs_axis = lax.axis_size("pair")
    me = lax.axis_index("orb") * pairs_axis + lax.axis_index("pair")
    npao, naux = own.shape[1:]
    norb = aux_hbm.shape[0]
    rest = npao - MAIN
    has = (me > 0, me < devices - 1)
    spot = lax.rem(me, 2 * pairs_axis)
    keeps = (
        jnp.logical_and(has[0], spot >= pairs_axis),
        jnp.logical_and(
            has[1], jnp.logical_or(spot < pairs_axis - 1, spot == 2 * pairs_axis - 1)
        ),
    )
    gives = tuple(jnp.logical_and(h, jnp.logical_not(k)) for h, k in zip(has, keeps))
    peers = tuple(
        (lax.div(at, pairs_axis), lax.rem(at, pairs_axis))
        for at in (lax.rem(me + devices - 1, devices), lax.rem(me + 1, devices))
    )

    groups = norb // 8
    group = me // 2
    aux_start = (group - 1) * 8
    loads = [
        pltpu.make_async_copy(src, dst, local_sems.at[n])
        for n, (src, dst) in enumerate(
            (
                (pao_hbm, pao_window),
                (amps_hbm, raw),
                (blocks_hbm, own),
                (gap_hbm, gap_window),
                (blocks_hbm, blocks.at[1]),
                *[
                    (
                        aux_hbm.at[pl.ds(lax.rem(group + groups - 1 + g, groups) * 8, 8)],
                        aux.at[8 * g : 8 * g + 8],
                    )
                    for g in range(3)
                ],
            )
        )
    ]
    for copy in loads:
        copy.start()

    barrier = pltpu.get_barrier_semaphore()
    for side in range(2):

        @pl.when(has[side])
        def _(side=side):
            pl.semaphore_signal(barrier, inc=1, device_id=peers[side], device_id_type=MESH)

    inner = jnp.logical_and(*has)

    @pl.when(inner)
    def _():
        pl.semaphore_wait(barrier, 2)

    @pl.when(jnp.logical_not(inner))
    def _():
        pl.semaphore_wait(barrier, 1)

    def remote(n, side, back):
        number = n if isinstance(n, int) else -1
        half = npao // 2
        if number == AMPS:
            src, dst = amps.at[1], amps.at[2 - 2 * side]
        elif number in (BACK + LAST, LAST_BACK_LOW):
            rows = slice(0, half) if number == BACK + LAST else slice(half, npao)
            src, dst = result_out.at[side, LAST, rows], result_in.at[1 - side, LAST, rows]
        elif number in (LAST, LAST_LOW):
            rows = slice(0, half) if number == LAST else slice(half, npao)
            src, dst = blocks_hbm.at[LAST, rows], blocks.at[2 - 2 * side, LAST, rows]
        elif back:
            src, dst = result_out.at[side, n - BACK], result_in.at[1 - side, n - BACK]
        else:
            src, dst = blocks_hbm.at[n], blocks.at[2 - 2 * side, n]
        return pltpu.make_async_remote_copy(
            src_ref=src,
            dst_ref=dst,
            send_sem=send_sems.at[n, side],
            recv_sem=recv_sems.at[n, side],
            device_id=peers[side],
            device_id_type=MESH,
        )

    def each(senders, act, back=False):
        for side in range(2):

            @pl.when(senders[side])
            def _(side=side):
                act(side, back)

    def start(n, senders, back=False):
        each(senders, lambda side, back: remote(n, side, back).start(), back)

    def sent(n, senders, back=False):
        each(senders, lambda side, back: remote(n, side, back).wait_send(), back)

    def arrived(n, receivers, back=False):
        each(receivers, lambda side, back: remote(n, 1 - side, back).wait_recv(), back)

    start(0, gives)

    def rows_of(window):
        x = window[...]
        return jnp.concatenate([x, x[MAIN:]], axis=0).T

    loads[0].wait()
    tab[...] = rows_of(pao_window)
    loads[1].wait()
    first = me * OCC_DEV

    @pl.loop(0, OCC_DEV)
    def _(k):
        left = column(tab[pl.ds(first + k, 1), :], npao)[:, :1] >= 0
        tails = []
        for n in range(2):
            p = k + n * OCC_DEV
            at = partner[me * PAIR_DEV + p]
            keep = left & (tab[pl.ds(at, 1), :] >= 0)[:, :npao]
            amp = jnp.where(keep, raw[p].astype(F32), F32(0))
            amps[1, k, :, n * MAIN : (n + 1) * MAIN] = amp[:, :MAIN].astype(BF16)
            tails.append(amp[:, MAIN:])
        amps[1, k, :, 2 * MAIN :] = jnp.concatenate(tails, axis=1).astype(BF16)

    loads[3].wait()
    gap[...] = rows_of(gap_window)
    for side in range(2):

        @pl.when(jnp.logical_not(has[side]))
        def _(side=side):
            amps[2 * side] = jnp.zeros_like(amps[2 * side])

    start(AMPS, has)
    loads[2].wait()
    for g in range(3):
        loads[5 + g].wait()

    def aligned(out, o, other):
        col = column(aux[pl.ds(me * OCC_DEV + o - aux_start, 1), :], naux)
        present = aux[pl.ds(other, 1), :]
        for at in range(0, naux, MAIN):
            pick = lanes(col, present[:, at : at + MAIN])
            out[:, at : at + MAIN] = dot(own[o], pick).astype(BF16)

    def align(p):
        second = wrapped(partner[me * PAIR_DEV + p] - aux_start, aux.shape[0])
        aligned(picked.at[p], lax.rem(p, OCC_DEV), second)

    pl.loop(0, 1)(align)
    for side in range(2):

        @pl.when(keeps[side])
        def _(side=side):
            far = me - 1 + 2 * side

            @pl.loop(0, PAIR_DEV)
            def _(p):
                o = wrapped(partner[far * PAIR_DEV + p] - me * OCC_DEV, OCC_DEV)
                first = far * OCC_DEV + lax.rem(p, OCC_DEV) - aux_start
                aligned(turned.at[side, p], o, first)

    pl.loop(1, PAIR_DEV // 2)(align)
    busy = jnp.logical_and(*keeps)

    @pl.when(jnp.logical_not(busy))
    def _():
        pl.loop(PAIR_DEV // 2, PAIR_DEV)(align)

    def exchange_back(k, lo=0, hi=npao):
        for side in range(2):

            @pl.when(keeps[side])
            def _(side=side):
                tails = []
                for n in range(2):
                    whole = dot(
                        blocks[2 * side, k, lo:hi], turned[side, k + n * OCC_DEV], CONTRACT_LAST
                    )
                    at = slice(n * MAIN, (n + 1) * MAIN)
                    result_out[side, k, lo:hi, at] = whole[:, :MAIN].astype(BF16)
                    tails.append(whole[:, MAIN:])
                result_out[side, k, lo:hi, 2 * MAIN :] = jnp.concatenate(tails, axis=1).astype(BF16)

    def amp_of(side, p):
        k, half = lax.rem(p, OCC_DEV), lax.div(p, OCC_DEV)
        main = amps[side, k, :, pl.ds(pl.multiple_of(half * MAIN, MAIN), MAIN)]
        tail = amps[side, k, :, 2 * MAIN :].astype(F32)
        tail = jnp.where(half == 0, tail, pltpu.roll(tail, rest, 1))
        return main, tail[:, :rest]

    def right_terms(side, first=0, last=PAIR_DEV):
        @pl.loop(first, last)
        def _(p):
            q = lax.rem((me + devices - 1 + side) * PAIR_DEV + p, devices * PAIR_DEV)
            target = partner[q] - me * OCC_DEV
            main, tail = amp_of(side, p)
            whole = jnp.concatenate([main, tail.astype(BF16)], axis=1)
            term = dot(whole, whole, CONTRACT_FIRST)
            for o in range(OCC_DEV):
                acc[o] += jnp.where(target == o, F32(1), F32(0)) * term

    for o in range(OCC_DEV):
        packed = amps[1, o]
        acc[o] = dot(packed, packed, CONTRACT_LAST)
    right_terms(1)

    arrived(0, keeps)
    exchange_back(0)
    start(1, gives)
    sent(AMPS, has)
    start(2, gives)
    arrived(AMPS, has)
    low = lax.broadcasted_iota(jnp.int32, (1, 2 * rest), 1) < rest

    def couple(p):
        i_row = me * OCC_DEV + lax.rem(p, OCC_DEV)
        j_row = partner[me * PAIR_DEV + p]
        left = column(wanted(tab[pl.ds(i_row, 1), :]), npao)
        right = column(wanted(tab[pl.ds(j_row, 1), :]), npao)
        held_rest, held_row = None, None
        for c in range(NCPL):
            m = near[c, p]
            spot = wrapped(m - (me - 1) * PAIR_DEV, 3 * PAIR_DEV)
            side, inner = lax.div(spot, PAIR_DEV), lax.rem(spot, PAIR_DEV)
            slot, half = lax.rem(inner, OCC_DEV), lax.div(inner, OCC_DEV)
            i_m = lax.div(m, PAIR_DEV) * OCC_DEV + slot
            j_m = partner[m]
            scale = coef[c, p]
            pick = lanes(left, tab[pl.ds(i_m, 1), :])[:, :npao]
            both = amps[side, slot]
            main = jnp.where(half == 0, both[:, :MAIN], both[:, MAIN : 2 * MAIN])
            tail = both[:, 2 * MAIN :]
            rows_ref[:, c * MAIN : (c + 1) * MAIN] = (dot(pick, main) * scale).astype(BF16)
            got = dot(pick, tail) * scale
            got = jnp.where(half == c % 2, got, pltpu.roll(got, rest, 1))
            row = tab[pl.ds(j_m, 1), :]
            cols_ref[:, c * MAIN : (c + 1) * MAIN] = lanes(right, row[:, :MAIN])
            row = row[:, MAIN:]
            if c % 2 == 0:
                held_rest, held_row = got, row
            else:
                at = NCPL * MAIN + (c // 2) * 2 * rest
                rows_ref[:, at : at + 2 * rest] = jnp.where(low, held_rest, got).astype(BF16)
                cols_ref[:, at : at + 2 * rest] = lanes(right, jnp.where(low, held_row, row))
        coupling = dot(rows_ref[...], cols_ref[...], CONTRACT_LAST)
        gap_left = column(gap[pl.ds(i_row, 1), :], npao)[:, :1]
        gap_right = gap[pl.ds(j_row, 1), :]
        keep_right = tab[pl.ds(j_row, 1), :] >= 0
        main, tail = amp_of(1, p)
        for lo, hi, amp in ((0, MAIN, main.astype(F32)), (MAIN, npao, tail)):
            keep = (left[:, :1] >= 0) & keep_right[:, lo:hi]
            denom = gap_left + gap_right[:, lo:hi]
            half_inverse = 0.5 / denom
            scale_ref[p, :, lo:hi] = jnp.where(keep, half_inverse, F32(0))
            base_ref[p, :, lo:hi] = amp - (denom * amp - coupling[:, lo:hi]) * half_inverse

    pl.loop(0, 1)(couple)
    start(BACK, keeps, True)
    pl.loop(1, 4)(couple)
    sent(1, gives)
    start(3, gives)
    pl.loop(4, 5)(couple)
    arrived(1, keeps)
    exchange_back(1)
    pl.loop(5, 6)(couple)
    start(BACK + 1, keeps, True)
    arrived(2, keeps)
    exchange_back(2)
    pl.loop(6, 7)(couple)
    start(BACK + 2, keeps, True)
    sent(2, gives)
    start(LAST_LOW, gives)
    pl.loop(7, 8)(couple)
    right_terms(0)
    loads[4].wait()
    arrived(LAST, keeps)
    exchange_back(LAST, 0, npao // 2)
    right_terms(2, 0, 2)
    start(BACK + LAST, keeps, True)
    right_terms(2, 2, PAIR_DEV)
    acc[...] = acc[...] / npao

    def finish(k, parts=(0, 1)):
        for n in parts:
            p = k + n * OCC_DEV
            spot = wrapped(partner[me * PAIR_DEV + p] - (me - 1) * OCC_DEV, 3 * OCC_DEV)
            side, slot = lax.div(spot, OCC_DEV), lax.rem(spot, OCC_DEV)
            whole = dot(picked[p], blocks[side, slot], CONTRACT_LAST)
            amp = amps[1, k]
            tail = amp[:, 2 * MAIN + n * rest : 2 * MAIN + (n + 1) * rest].astype(F32)
            energy = F32(0)
            for lo, hi, at, value in (
                (0, MAIN, n * MAIN, amp[:, n * MAIN : (n + 1) * MAIN].astype(F32)),
                (MAIN, npao, 2 * MAIN + n * rest, tail),
            ):
                exchange = whole[:, lo:hi]
                for far in range(2):
                    came = jnp.logical_and(gives[far], side == 2 * far)
                    other = result_in[far, k, :, at : at + hi - lo].astype(F32)
                    exchange = jnp.where(came, other, exchange)
                new[p, :, lo:hi] = (
                    base_ref[p, :, lo:hi] - scale_ref[p, :, lo:hi] * exchange
                ).astype(BF16)
                energy += jnp.sum(exchange * value)
            energy_ref[pl.ds(p, 1), :] = jnp.full((1, LANE), energy / npao, F32)

    for k in range(LAST):
        arrived(BACK + k, gives, True)

    arrived(LAST_LOW, keeps)
    exchange_back(LAST, npao // 2, npao)
    pl.loop(0, 1)(lambda k: finish(k, (0,)))
    start(LAST_BACK_LOW, keeps, True)

    @pl.when(busy)
    def _():
        pl.loop(PAIR_DEV // 2, PAIR_DEV)(align)

    pl.loop(0, 1)(lambda k: finish(k, (1,)))
    pl.loop(1, LAST)(finish)
    arrived(BACK + LAST, gives, True)
    arrived(LAST_BACK_LOW, gives, True)
    pl.loop(LAST, OCC_DEV)(finish)
    sent(0, gives)
    sent(LAST, gives)
    sent(LAST_LOW, gives)
    for k in range(OCC_DEV):
        sent(BACK + k, keeps, True)
    sent(LAST_BACK_LOW, keeps, True)


def write_kernel(new, energy, dens, new_hbm, energy_out, dens_hbm, sems):
    half = new.shape[1] // 2
    pieces = [(new, new_hbm, p) for p in range(PAIR_DEV)]
    pieces += [(dens, dens_hbm, o) for o in range(OCC_DEV)]
    copies = [
        pltpu.make_async_copy(
            src.at[n, part * half : (part + 1) * half],
            dst.at[n, part * half : (part + 1) * half],
            sems.at[2 * at + part],
        )
        for at, (src, dst, n) in enumerate(pieces)
        for part in range(2)
    ]
    for copy in copies:
        copy.start()
    for p in range(PAIR_DEV):
        energy_out[p] = energy[p, 0]
    for copy in copies:
        copy.wait()


def local(
    blocks, aux_domain, pao_domain, pao_gap, amplitudes, pair_partner, coupling_list, coupling_coef
):
    devices = lax.axis_size(("orb", "pair"))
    naux, npao = blocks.shape[1:]
    norb = aux_domain.shape[0]
    hbm = pl.BlockSpec(memory_space=pltpu.MemorySpace.HBM)
    smem = pl.BlockSpec(memory_space=pltpu.MemorySpace.SMEM)
    vmem = pl.BlockSpec(memory_space=pltpu.MemorySpace.VMEM)
    sds = jax.ShapeDtypeStruct
    new_amps, energies, densities = pl.pallas_call(
        functools.partial(kernel, devices),
        out_shape=[
            pltpu.VMEM((PAIR_DEV, npao, npao), BF16),
            pltpu.VMEM((PAIR_DEV, LANE), F32),
            pltpu.VMEM((OCC_DEV, npao, npao), F32),
        ],
        in_specs=[smem] * 3 + [hbm] * 5,
        out_specs=[vmem, vmem, vmem],
        scratch_shapes=[
            pltpu.VMEM((OCC_DEV, npao, naux), BF16),
            pltpu.VMEM((24, naux), jnp.int32),
            pltpu.VMEM((npao, norb), jnp.int32),
            pltpu.VMEM((npao, norb), F32),
            pltpu.VMEM((PAIR_DEV, npao, npao), BF16),
            pltpu.VMEM((norb, 3 * LANE), jnp.int32),
            pltpu.VMEM((norb, 3 * LANE), F32),
            pltpu.VMEM((3, OCC_DEV, npao, 2 * npao), BF16),
            pltpu.VMEM((PAIR_DEV, npao, naux), BF16),
            pltpu.VMEM((2, PAIR_DEV, npao, naux), BF16),
            pltpu.VMEM((3, OCC_DEV, npao, naux), BF16),
            pltpu.VMEM((2, OCC_DEV, npao, 2 * npao), BF16),
            pltpu.VMEM((2, OCC_DEV, npao, 2 * npao), BF16),
            pltpu.VMEM((PAIR_DEV, npao, npao), F32),
            pltpu.VMEM((PAIR_DEV, npao, npao), F32),
            pltpu.VMEM((npao, NCPL * npao), BF16),
            pltpu.VMEM((npao, NCPL * npao), BF16),
            pltpu.SemaphoreType.DMA((8,)),
            pltpu.SemaphoreType.DMA((LAST_BACK_LOW + 1, 2)),
            pltpu.SemaphoreType.DMA((LAST_BACK_LOW + 1, 2)),
        ],
        compiler_params=pltpu.CompilerParams(
            collective_id=0, has_side_effects=True, vmem_limit_bytes=60 * 1024 * 1024
        ),
        name="update",
    )(
        pair_partner,
        coupling_list.T,
        coupling_coef.T,
        jnp.swapaxes(blocks, 1, 2),
        aux_domain,
        pao_domain.T,
        pao_gap.T,
        amplitudes,
    )
    return pl.pallas_call(
        write_kernel,
        out_shape=[
            sds((PAIR_DEV, npao, npao), BF16),
            sds((PAIR_DEV,), F32),
            sds((OCC_DEV, npao, npao), F32),
        ],
        in_specs=[vmem, vmem, vmem],
        out_specs=[hbm, smem, hbm],
        scratch_shapes=[pltpu.SemaphoreType.DMA((2 * (PAIR_DEV + OCC_DEV),))],
        compiler_params=pltpu.CompilerParams(vmem_limit_bytes=1024 * 1024),
        name="write",
    )(new_amps, energies, densities)


def solution(mesh):
    return jax.shard_map(
        local,
        mesh=mesh,
        in_specs=(
            P(("orb", "pair"), None, None),
            P(),
            P(),
            P(),
            P(("orb", "pair"), None, None),
            P(),
            P(("orb", "pair"), None),
            P(("orb", "pair"), None),
        ),
        out_specs=(
            P(("orb", "pair"), None, None),
            P(("orb", "pair")),
            P(("orb", "pair"), None, None),
        ),
        check_vma=False,
    )
```
